32 devices in a mesh: energy: 4 (over y, x), slab: 8 (over z, core).
Axes of the slice: x: 2, y: 2, z: 4, core: 2. Of those that a mesh axis runs over, the one named last changes fastest.
Arguments:
- left_basis: bfloat16 [8, 768, 768], P('slab'), may hold values from -0.21875 to 0.21875
- right_basis: bfloat16 [8, 768, 768], P('slab'), may hold values from -0.21875 to 0.21875
- potential_index: int32 [8], P('slab'), may hold values from 0 to 7
- levels: float32 [8, 768], replicated, may hold values from 0.8 to 1.25
- energy_values: float32 [64], replicated, may hold values from -0.1 to 0.1
- energy_weights: float32 [64], replicated, may hold values from 0.2 to 5
- energy_index: int32 [16], P('energy'), may hold values from 0 to 63
- left_source: bfloat16 [768, 128], replicated, may hold values from -6 to 6
- right_source: bfloat16 [768, 128], replicated, may hold values from -6 to 6
Outputs:
- density: float32 [8, 768], P('slab')
The draws below stay inside these ranges and needn't reach their ends.
All inputs are finite; a program needn't handle non-finite values.
Results may differ from the reference program's by a relative error of at most 0.0044.
Values may be sent and summed in bfloat16 or wider, within the bound.
A program may use at most 64 MiB of HBM per device.

```python
import math
import jax
import jax.numpy as jnp
from jax import lax

W = 768
M = 128
NPOT = 8
SLABS = 8
NE = 16
GRID = 64


def touch_ends(array, rng, low, top_value):
    index_at = [jax.random.randint(jax.random.fold_in(rng, axis), (), 0, length) for axis, length in enumerate(array.shape)]
    widest = array.shape.index(max(array.shape))
    next_to = index_at[:widest] + [(index_at[widest] + 1) % array.shape[widest]] + index_at[widest + 1:]
    return array.at[tuple(index_at)].set(low).at[tuple(next_to)].set(top_value)


def shard_levels(own_key, extent, cuts, smallest, high):
    def one(dim, shards_of):
        heights = jax.random.uniform(jax.random.fold_in(jax.random.fold_in(own_key, 6), dim), (shards_of,), jnp.float32, smallest / len(cuts), high / len(cuts))
        return jnp.repeat(jnp.exp(heights), extent[dim] // shards_of).reshape((-1,) + (1,) * (len(extent) - dim - 1))

    loudness = one(*cuts[0])
    for cut in cuts[1:]:
        loudness = loudness * one(*cut)
    return loudness


def centred(stream_key, shape, scale, bound, split=(), dtype=jnp.bfloat16):
    values = jax.random.normal(stream_key, shape, jnp.float32) * scale
    if len(split) > 0:
        values = shard_levels(stream_key, shape, split, -0.22, 0.18) * values
    return jnp.clip(values, min=-bound, max=bound).astype(dtype)


def setup_inputs(seed: int = 0) -> dict:
    streams_of = jax.random.split(jax.random.key(seed), 10)
    left_basis = centred(streams_of[0], (SLABS, W, W), W ** -0.5, 0.21875, ((0, 8),))
    right_basis = centred(streams_of[1], (SLABS, W, W), W ** -0.5, 0.21875, ((0, 8),))
    potential_index = touch_ends(jax.random.randint(streams_of[2], (SLABS,), 0, NPOT), jax.random.fold_in(streams_of[2], 1), 0, NPOT - 1).astype(jnp.int32)
    levels = jnp.clip(jax.random.uniform(streams_of[3], (NPOT, W), jnp.float32, 0.8, 1.25), 0.8, 1.25)
    energy_values = jnp.clip(jax.random.uniform(streams_of[4], (GRID,), jnp.float32, -0.1, 0.1), -0.1, 0.1)
    energy_weights = jnp.clip(jnp.exp(jax.random.uniform(streams_of[5], (GRID,), jnp.float32, math.log(0.2), math.log(5.0))), 0.2, 5.0)
    energy_index = touch_ends(jax.random.randint(streams_of[6], (NE,), 0, GRID), jax.random.fold_in(streams_of[6], 1), 0, GRID - 1).astype(jnp.int32)
    left_source = centred(streams_of[7], (W, M), 1.0, 6.0)
    right_source = centred(streams_of[8], (W, M), 1.0, 6.0)
    return {"left_basis": left_basis, "right_basis": right_basis, "potential_index": potential_index, "levels": levels, "energy_values": energy_values, "energy_weights": energy_weights, "energy_index": energy_index, "left_source": left_source, "right_source": right_source}


def reference(left_basis, right_basis, potential_index, levels, energy_values, energy_weights, energy_index, left_source, right_source):
    energy = energy_values[energy_index]
    weight = energy_weights[energy_index] / (NE * M)
    factors = 1.0 / (energy[None, :, None] - levels[potential_index][:, None, :])

    def density_of(state):
        return jnp.einsum('e,ewm->w', weight, state.astype(jnp.float32) ** 2)

    def down(state, item):
        lower, upper, scale = item
        mixed = jnp.einsum('vw,ewm->evm', upper.astype(jnp.float32), state.astype(jnp.float32))
        scaled = (scale[:, :, None] * mixed).astype(jnp.bfloat16)
        fresh = jnp.einsum('vw,ewm->evm', lower.astype(jnp.float32), scaled.astype(jnp.float32)).astype(jnp.bfloat16)
        return fresh, density_of(fresh)

    def back(state, item):
        lower, upper, scale = item
        mixed = jnp.einsum('wv,ewm->evm', lower.astype(jnp.float32), state.astype(jnp.float32))
        scaled = (scale[:, :, None] * mixed).astype(jnp.bfloat16)
        fresh = jnp.einsum('wv,ewm->evm', upper.astype(jnp.float32), scaled.astype(jnp.float32)).astype(jnp.bfloat16)
        return fresh, density_of(fresh)

    start_left = jnp.broadcast_to(left_source, (NE, W, M))
    start_right = jnp.broadcast_to(right_source, (NE, W, M))
    _, forward_part = lax.scan(down, start_left, (left_basis, right_basis, factors))
    _, backward_part = lax.scan(back, start_right, (left_basis, right_basis, factors), reverse=True)
    return forward_part + backward_part
```

```python
import functools

import jax
import jax.numpy as jnp
from jax import lax
from jax.experimental import pallas as pl
from jax.experimental.pallas import tpu as pltpu
from jax.sharding import PartitionSpec as P

MESH = pl.DeviceIdType.MESH
NN = (((1,), (0,)), ((), ()))
NT = (((1,), (1,)), ((), ()))


def dot(a, b, dims):
    return lax.dot_general(a, b, dims, preferred_element_type=jnp.float32)


def kernel(
    chain,
    teams,
    potential,
    energies_hbm,
    weights_hbm,
    indices_hbm,
    levels_hbm,
    left_source_hbm,
    right_source_hbm,
    left_hbm,
    right_hbm,
    out,
    energies,
    weights,
    indices,
    levels,
    source,
    left,
    right,
    left_turned,
    right_turned,
    joined,
    rows,
    first,
    kept,
    density,
    mine,
    extra,
    partial,
    gathered,
    forward_in,
    forward_out,
    backward_in,
    backward_out,
    load_sem,
    swap_send,
    swap_recv,
    forward_send,
    forward_recv,
    backward_send,
    backward_recv,
    extra_send,
    extra_recv,
    gather_send,
    gather_recv,
):
    count = indices.shape[0]
    modes = source.shape[1]
    orbitals = levels.shape[1]
    half = modes // 2
    spot = lax.axis_index("slab")
    team = lax.axis_index("energy")
    chips = chain // 2
    chip = spot // 2
    core = spot % 2
    twin = spot + 1 - 2 * core
    lowest = chip == 0
    highest = chip == chips - 1
    inner = jnp.logical_not(lowest | highest)
    upper = chip >= chips // 2
    speaker = jnp.where(highest, 0, 1)
    speaks = core == speaker

    def load(origin, target, place):
        return pltpu.make_async_copy(origin, target, load_sem.at[place])

    left_load = load(left_source_hbm, source, 0)
    right_load = load(right_source_hbm, source, 0)
    right_base = load(right_hbm.at[0], right.at[core], 1)
    left_base = load(left_hbm.at[0], left.at[core], 2)
    tables = [
        load(energies_hbm, energies, 3),
        load(weights_hbm, weights, 4),
        load(indices_hbm, indices, 5),
        load(levels_hbm, levels, 6),
    ]
    pl.when(spot == 0)(left_load.start)
    pl.when(spot == chain - 1)(right_load.start)
    left_base.start()
    for item in tables:
        item.start()
    right_base.start()

    barrier = pltpu.get_barrier_semaphore()

    def greet(place):
        pl.semaphore_signal(barrier, inc=1, device_id=place, device_id_type=MESH)

    greet({"slab": twin})
    pl.when((core == 0) & jnp.logical_not(lowest))(
        lambda: greet({"slab": jnp.where(chip == 1, 1, spot - 2)})
    )
    pl.when((core == 1) & jnp.logical_not(highest))(
        lambda: greet({"slab": jnp.where(chip == chips - 2, chain - 2, spot + 2)})
    )
    for step in range(1, teams):
        greet({"energy": lax.rem(team + step, teams), "slab": 2 * chip + speaker})
    sends_forward = jnp.where(lowest, core == 1, (core == 0) & jnp.logical_not(highest))
    sends_backward = jnp.where(highest, core == 0, (core == 1) & jnp.logical_not(lowest))
    greetings = (
        1
        + sends_forward.astype(jnp.int32)
        + sends_backward.astype(jnp.int32)
        + jnp.where(speaks, 2 * (teams - 1), 0)
    )

    density[...] = jnp.zeros_like(density)
    for item in tables:
        item.wait()
    rows[core] = levels[pl.ds(potential[0], 1), :]

    def swap(origin, target, place):
        return pltpu.make_async_remote_copy(
            src_ref=origin,
            dst_ref=target,
            send_sem=swap_send.at[place],
            recv_sem=swap_recv.at[place],
            device_id={"slab": twin},
            device_id_type=MESH,
        )

    swap_rows = swap(rows.at[core], rows.at[core], 0)
    swap_right = swap(right_hbm.at[0], right.at[core], 1)
    swap_left = swap(left_hbm.at[0], left.at[core], 2)

    def start_swaps():
        swap_rows.start()

        @pl.when(core == 0)
        def _():
            swap_left.start()
            swap_right.start()

        @pl.when(core == 1)
        def _():
            swap_right.start()
            swap_left.start()

    def settle_bases():
        right_base.wait()
        left_base.wait()

    def turned_source():
        return source[...].astype(jnp.float32).T.astype(jnp.bfloat16)

    def turn_bases(side):
        left_turned[side] = left[side].T
        right_turned[side] = right[side].T

    @pl.when(spot == 0)
    def _():
        settle_bases()
        left_load.wait()
        first[...] = dot(turned_source(), right[0], NT)

    @pl.when(spot == chain - 1)
    def _():
        right_load.wait()
        left_base.wait()
        first[...] = dot(turned_source(), left[1], NN)
        right_base.wait()

    @pl.when(spot == 1)
    def _():
        settle_bases()
        turn_bases(1)

    pl.when(spot == chain - 2)(settle_bases)
    pl.semaphore_wait(barrier, greetings)

    @pl.when(inner)
    def _():
        start_swaps()
        settle_bases()

    def forward_copy(slot, place):
        return pltpu.make_async_remote_copy(
            src_ref=forward_out.at[slot],
            dst_ref=forward_in.at[slot],
            send_sem=forward_send.at[slot],
            recv_sem=forward_recv.at[slot],
            device_id={"slab": place},
            device_id_type=MESH,
        )

    def backward_copy(slot, part, place):
        return pltpu.make_async_remote_copy(
            src_ref=backward_out.at[slot, part],
            dst_ref=backward_in.at[slot, part],
            send_sem=backward_send.at[slot, part],
            recv_sem=backward_recv.at[slot, part],
            device_id={"slab": place},
            device_id_type=MESH,
        )

    def scaled(mixed, slot, side):
        scale = 1.0 / (energies[indices[slot]] - rows[side])
        return (scale * mixed).astype(jnp.bfloat16)

    def count_in(state, slot, side):
        weight = weights[indices[slot]] / (count * teams * modes)
        squared = state.astype(jnp.float32) ** 2
        part = jnp.sum(squared.reshape(-1, 8, orbitals), axis=0)
        density[side] += weight * part

    def down(state, slot, side):
        mixed = dot(state, right_turned[side], NN)
        return dot(scaled(mixed, slot, side), left_turned[side], NN).astype(jnp.bfloat16)

    def up(state, slot, side):
        mixed = dot(state, left[side], NN)
        return dot(scaled(mixed, slot, side), right[side], NN).astype(jnp.bfloat16)

    def each(body):
        def step(slot, carry):
            body(slot)
            return carry

        lax.fori_loop(0, count, step, 0)

    @pl.when(spot == 0)
    def _():
        def body(slot):
            fresh = dot(scaled(first[...], slot, 0), left[0], NT).astype(jnp.bfloat16)
            forward_out[slot] = fresh
            forward_copy(slot, twin).start()
            count_in(fresh, slot, 0)

        each(body)
        start_swaps()

    @pl.when(spot == 1)
    def _():
        def body(slot):
            forward_copy(slot, twin).wait_recv()
            fresh = down(forward_in[slot], slot, 1)
            forward_out[slot] = fresh
            forward_copy(slot, 2).start()
            count_in(fresh, slot, 1)

        each(body)

    @pl.when(spot == chain - 1)
    def _():
        def body(slot):
            fresh = dot(scaled(first[...], slot, 1), right[1], NN).astype(jnp.bfloat16)
            for part in range(2):
                backward_out[slot, part] = fresh[part * half : (part + 1) * half]
                backward_copy(slot, part, twin).start()
            count_in(fresh, slot, 1)

        each(body)
        start_swaps()

    @pl.when(spot == chain - 2)
    def _():
        def body(slot):
            for part in range(2):
                backward_copy(slot, part, twin).wait_recv()
                fresh = up(backward_in[slot, part], slot, 0)
                backward_out[slot, part] = fresh
                backward_copy(slot, part, chain - 3).start()
                count_in(fresh, slot, 0)

        each(body)

    def fold(side):
        return jnp.sum(density[side], axis=0, keepdims=True)

    hand_over = pltpu.make_async_remote_copy(
        src_ref=mine,
        dst_ref=extra,
        send_sem=extra_send.at[0],
        recv_sem=extra_recv.at[0],
        device_id={"slab": twin},
        device_id_type=MESH,
    )

    @pl.when((core == 0) & jnp.logical_not(lowest))
    def _():
        turn_bases(0)
        swap_rows.wait_recv()
        swap_right.wait_recv()
        swap_left.wait_recv()
        turn_bases(1)

        def body(slot):
            forward_copy(slot, twin).wait_recv()
            between = down(forward_in[slot], slot, 0)
            fresh = down(between, slot, 1)
            forward_out[slot] = fresh
            pl.when(inner)(lambda: forward_copy(slot, spot + 2).start())
            count_in(between, slot, 0)
            count_in(fresh, slot, 1)

        each(body)

    def count_kept(slot):
        fresh = dot(kept[...], right[1], NN).astype(jnp.bfloat16)
        count_in(fresh, slot, 1)

    @pl.when((core == 1) & jnp.logical_not(highest))
    def _():
        swap_rows.wait_recv()
        swap_left.wait_recv()
        joined[...] = dot(right[1], left[0], NN).astype(jnp.bfloat16)
        swap_right.wait_recv()

        def body(slot):
            pl.when(slot > 0)(lambda: count_kept(slot - 1))
            for part in range(2):
                backward_copy(slot, part, twin).wait_recv()
                upper_mix = scaled(dot(backward_in[slot, part], left[1], NN), slot, 1)
                kept[part * half : (part + 1) * half] = upper_mix
                lower_mix = scaled(dot(upper_mix, joined[...], NN), slot, 0)
                fresh = dot(lower_mix, right[0], NN).astype(jnp.bfloat16)
                backward_out[slot, part] = fresh
                pl.when(inner)(lambda: backward_copy(slot, part, spot - 2).start())
                count_in(fresh, slot, 0)

        each(body)

    def share(side, step):
        return pltpu.make_async_remote_copy(
            src_ref=partial.at[side],
            dst_ref=gathered.at[team],
            send_sem=gather_send.at[side, step],
            recv_sem=gather_recv.at[step],
            device_id={"energy": lax.rem(team + step, teams), "slab": 2 * chip + side},
            device_id_type=MESH,
        )

    def speak(side):
        partial[side] = fold(side) + extra[side]
        for step in range(1, teams):
            share(side, step).start()
        pl.when(core != side)(share(side, 0).start)

        @pl.when(core == side)
        def _():
            gathered[team] = partial[side]

    @pl.when(jnp.logical_not(speaks))
    def _():
        for side in range(2):
            mine[side] = fold(side)
        hand_over.start()

    @pl.when(speaks)
    def _():
        hand_over.wait_recv()
        speak(0)

    pl.when((core == 1) & jnp.logical_not(highest))(lambda: count_kept(count - 1))
    pl.when(speaks)(lambda: speak(1))

    pl.when(sends_forward | (spot == 0))(
        lambda: each(lambda slot: forward_copy(slot, twin).wait_send())
    )

    @pl.when(sends_backward | (spot == chain - 1))
    def _():
        for part in range(2):
            each(lambda slot: backward_copy(slot, part, twin).wait_send())

    @pl.when(inner | (spot == 0) | (spot == chain - 1))
    def _():
        swap_rows.wait_send()
        swap_right.wait_send()
        swap_left.wait_send()

    pl.when(jnp.logical_not(speaks))(hand_over.wait_send)

    @pl.when(speaks)
    def _():
        for side in range(2):
            for step in range(1, teams):
                share(side, step).wait_send()
            pl.when(core != side)(share(side, 0).wait_send)

    pl.when(jnp.logical_not(speaks))(share(0, 0).wait_recv)
    for step in range(1, teams):
        share(0, step).wait_recv()
    total = gathered[0]
    for member in range(1, teams):
        total += gathered[member]
    out[...] = total


def local(
    teams,
    chain,
    left_basis,
    right_basis,
    potential_index,
    levels,
    energy_values,
    energy_weights,
    energy_index,
    left_source,
    right_source,
):
    count = energy_index.shape[0]
    orbitals = left_basis.shape[1]
    modes = left_source.shape[1]
    outside = pl.BlockSpec(memory_space=pltpu.HBM)
    square = pltpu.VMEM((2, orbitals, orbitals), jnp.bfloat16)
    pair = pltpu.VMEM((2, 1, orbitals), jnp.float32)
    return pl.pallas_call(
        functools.partial(kernel, chain, teams),
        out_shape=jax.ShapeDtypeStruct((1, orbitals), jnp.float32),
        in_specs=[pl.BlockSpec(memory_space=pltpu.SMEM)] + [outside] * 8,
        out_specs=pl.BlockSpec(memory_space=pltpu.VMEM),
        scratch_shapes=[
            pltpu.SMEM(energy_values.shape, jnp.float32),
            pltpu.SMEM(energy_weights.shape, jnp.float32),
            pltpu.SMEM(energy_index.shape, jnp.int32),
            pltpu.VMEM(levels.shape, jnp.float32),
            pltpu.VMEM(left_source.shape, jnp.bfloat16),
            square,
            square,
            square,
            square,
            pltpu.VMEM((orbitals, orbitals), jnp.bfloat16),
            pltpu.VMEM((2, 1, orbitals), jnp.float32),
            pltpu.VMEM((modes, orbitals), jnp.float32),
            pltpu.VMEM((modes, orbitals), jnp.bfloat16),
            pltpu.VMEM((2, 8, orbitals), jnp.float32),
            pair,
            pair,
            pair,
            pltpu.VMEM((teams, 1, orbitals), jnp.float32),
            pltpu.VMEM((count, modes, orbitals), jnp.bfloat16),
            pltpu.VMEM((count, modes, orbitals), jnp.bfloat16),
            pltpu.VMEM((count, 2, modes // 2, orbitals), jnp.bfloat16),
            pltpu.VMEM((count, 2, modes // 2, orbitals), jnp.bfloat16),
            pltpu.SemaphoreType.DMA((7,)),
            pltpu.SemaphoreType.DMA((3,)),
            pltpu.SemaphoreType.DMA((3,)),
            pltpu.SemaphoreType.DMA((count,)),
            pltpu.SemaphoreType.DMA((count,)),
            pltpu.SemaphoreType.DMA((count, 2)),
            pltpu.SemaphoreType.DMA((count, 2)),
            pltpu.SemaphoreType.DMA((1,)),
            pltpu.SemaphoreType.DMA((1,)),
            pltpu.SemaphoreType.DMA((2, teams)),
            pltpu.SemaphoreType.DMA((teams,)),
        ],
        compiler_params=pltpu.CompilerParams(
            collective_id=0, has_side_effects=True, vmem_limit_bytes=63 << 20
        ),
    )(
        potential_index,
        energy_values,
        energy_weights,
        energy_index,
        levels,
        left_source,
        right_source,
        left_basis,
        right_basis,
    )


def solution(mesh):
    placed = (
        P("slab", None, None),
        P("slab", None, None),
        P("slab"),
        P(),
        P(),
        P(),
        P("energy"),
        P(),
        P(),
    )
    return jax.shard_map(
        functools.partial(local, mesh.shape["energy"], mesh.shape["slab"]),
        mesh=mesh,
        in_specs=placed,
        out_specs=P("slab", None),
        check_vma=False,
    )
```

```python
import functools

import jax
import jax.numpy as jnp
from jax import lax
from jax.experimental import pallas as pl
from jax.experimental.pallas import tpu as pltpu
from jax.sharding import PartitionSpec as P

MESH = pl.DeviceIdType.MESH
NN = (((1,), (0,)), ((), ()))
NT = (((1,), (1,)), ((), ()))


def dot(a, b, dims):
    return lax.dot_general(a, b, dims, preferred_element_type=jnp.float32)


def kernel(
    chain,
    teams,
    potential_hbm,
    energies_hbm,
    weights_hbm,
    indices_hbm,
    levels_hbm,
    left_source_hbm,
    right_source_hbm,
    left_hbm,
    right_hbm,
    out,
    potential,
    energies,
    weights,
    indices,
    levels,
    source,
    left,
    right,
    left_turned,
    right_turned,
    joined,
    rows,
    first,
    kept,
    density,
    mine,
    extra,
    partial,
    gathered,
    forward_in,
    forward_out,
    backward_in,
    backward_out,
    load_sem,
    swap_send,
    swap_recv,
    forward_send,
    forward_recv,
    backward_send,
    backward_recv,
    extra_send,
    extra_recv,
    gather_send,
    gather_recv,
):
    count = indices.shape[0]
    modes = source.shape[1]
    orbitals = levels.shape[1]
    half = modes // 2
    spot = lax.axis_index("slab")
    team = lax.axis_index("energy")
    chips = chain // 2
    chip = spot // 2
    core = spot % 2
    twin = spot + 1 - 2 * core
    lowest = chip == 0
    highest = chip == chips - 1
    inner = jnp.logical_not(lowest | highest)
    upper = chip >= chips // 2
    speaker = jnp.where(highest, 0, 1)
    speaks = core == speaker

    def load(origin, target, place):
        return pltpu.make_async_copy(origin, target, load_sem.at[place])

    left_load = load(left_source_hbm, source, 0)
    right_load = load(right_source_hbm, source, 0)
    right_base = load(right_hbm.at[0], right.at[core], 1)
    left_base = load(left_hbm.at[0], left.at[core], 2)
    tables = [
        load(energies_hbm, energies, 3),
        load(weights_hbm, weights, 4),
        load(indices_hbm, indices, 5),
        load(levels_hbm, levels, 6),
        load(potential_hbm, potential, 7),
    ]
    pl.when(spot == 0)(left_load.start)
    pl.when(spot == chain - 1)(right_load.start)
    left_base.start()
    for item in tables:
        item.start()
    right_base.start()

    barrier = pltpu.get_barrier_semaphore()

    def greet(place):
        pl.semaphore_signal(barrier, inc=1, device_id=place, device_id_type=MESH)

    greet({"slab": twin})
    pl.when((core == 0) & jnp.logical_not(lowest))(
        lambda: greet({"slab": jnp.where(chip == 1, 1, spot - 2)})
    )
    pl.when((core == 1) & jnp.logical_not(highest))(
        lambda: greet({"slab": jnp.where(chip == chips - 2, chain - 2, spot + 2)})
    )
    for step in range(1, teams):
        greet({"energy": lax.rem(team + step, teams), "slab": 2 * chip + speaker})
    sends_forward = jnp.where(lowest, core == 1, (core == 0) & jnp.logical_not(highest))
    sends_backward = jnp.where(highest, core == 0, (core == 1) & jnp.logical_not(lowest))
    greetings = (
        1
        + sends_forward.astype(jnp.int32)
        + sends_backward.astype(jnp.int32)
        + jnp.where(speaks, 2 * (teams - 1), 0)
    )

    density[...] = jnp.zeros_like(density)
    for item in tables:
        item.wait()
    rows[core] = levels[pl.ds(potential[0], 1), :]

    def swap(origin, target, place):
        return pltpu.make_async_remote_copy(
            src_ref=origin,
            dst_ref=target,
            send_sem=swap_send.at[place],
            recv_sem=swap_recv.at[place],
            device_id={"slab": twin},
            device_id_type=MESH,
        )

    swap_rows = swap(rows.at[core], rows.at[core], 0)
    swap_right = swap(right_hbm.at[0], right.at[core], 1)
    swap_left = swap(left_hbm.at[0], left.at[core], 2)

    def start_swaps():
        swap_rows.start()

        @pl.when(core == 0)
        def _():
            swap_left.start()
            swap_right.start()

        @pl.when(core == 1)
        def _():
            swap_right.start()
            swap_left.start()

    def settle_bases():
        right_base.wait()
        left_base.wait()

    def turned_source():
        return source[...].astype(jnp.float32).T.astype(jnp.bfloat16)

    def turn_bases(side):
        left_turned[side] = left[side].T
        right_turned[side] = right[side].T

    @pl.when(spot == 0)
    def _():
        settle_bases()
        left_load.wait()
        first[...] = dot(turned_source(), right[0], NT)

    @pl.when(spot == chain - 1)
    def _():
        right_load.wait()
        left_base.wait()
        first[...] = dot(turned_source(), left[1], NN)
        right_base.wait()

    @pl.when(spot == 1)
    def _():
        settle_bases()
        turn_bases(1)

    pl.when(spot == chain - 2)(settle_bases)
    pl.semaphore_wait(barrier, greetings)

    @pl.when(inner)
    def _():
        start_swaps()
        settle_bases()

    def forward_copy(slot, part, place):
        return pltpu.make_async_remote_copy(
            src_ref=forward_out.at[slot, part],
            dst_ref=forward_in.at[slot, part],
            send_sem=forward_send.at[slot, part],
            recv_sem=forward_recv.at[slot, part],
            device_id={"slab": place},
            device_id_type=MESH,
        )

    def backward_copy(slot, part, place):
        return pltpu.make_async_remote_copy(
            src_ref=backward_out.at[slot, part],
            dst_ref=backward_in.at[slot, part],
            send_sem=backward_send.at[slot, part],
            recv_sem=backward_recv.at[slot, part],
            device_id={"slab": place},
            device_id_type=MESH,
        )

    def scaled(mixed, slot, side):
        scale = 1.0 / (energies[indices[slot]] - rows[side])
        return (scale * mixed).astype(jnp.bfloat16)

    def count_in(state, slot, side):
        weight = weights[indices[slot]] / (count * teams * modes)
        squared = state.astype(jnp.float32) ** 2
        part = jnp.sum(squared.reshape(-1, 8, orbitals), axis=0)
        density[side] += weight * part

    def down(state, slot, side):
        mixed = dot(state, right_turned[side], NN)
        return dot(scaled(mixed, slot, side), left_turned[side], NN).astype(jnp.bfloat16)

    def up(state, slot, side):
        mixed = dot(state, left[side], NN)
        return dot(scaled(mixed, slot, side), right[side], NN).astype(jnp.bfloat16)

    def each(body):
        def step(slot, carry):
            body(slot)
            return carry

        lax.fori_loop(0, count, step, 0)

    @pl.when(spot == 0)
    def _():
        def body(slot):
            fresh = dot(scaled(first[...], slot, 0), left[0], NT).astype(jnp.bfloat16)
            for part in range(2):
                forward_out[slot, part] = fresh[part * half : (part + 1) * half]
                forward_copy(slot, part, twin).start()
            count_in(fresh, slot, 0)

        each(body)
        start_swaps()

    @pl.when(spot == 1)
    def _():
        def body(slot):
            for part in range(2):
                forward_copy(slot, part, twin).wait_recv()
                fresh = down(forward_in[slot, part], slot, 1)
                forward_out[slot, part] = fresh
                forward_copy(slot, part, 2).start()
                count_in(fresh, slot, 1)

        each(body)

    @pl.when(spot == chain - 1)
    def _():
        def body(slot):
            fresh = dot(scaled(first[...], slot, 1), right[1], NN).astype(jnp.bfloat16)
            for part in range(2):
                backward_out[slot, part] = fresh[part * half : (part + 1) * half]
                backward_copy(slot, part, twin).start()
            count_in(fresh, slot, 1)

        each(body)
        start_swaps()

    @pl.when(spot == chain - 2)
    def _():
        def body(slot):
            for part in range(2):
                backward_copy(slot, part, twin).wait_recv()
                fresh = up(backward_in[slot, part], slot, 0)
                backward_out[slot, part] = fresh
                backward_copy(slot, part, chain - 3).start()
                count_in(fresh, slot, 0)

        each(body)

    def count_lower(slot):
        fresh = dot(kept[...], left_turned[0], NN).astype(jnp.bfloat16)
        count_in(fresh, slot, 0)

    def fold(side):
        return jnp.sum(density[side], axis=0, keepdims=True)

    hand_over = pltpu.make_async_remote_copy(
        src_ref=mine,
        dst_ref=extra,
        send_sem=extra_send.at[0],
        recv_sem=extra_recv.at[0],
        device_id={"slab": twin},
        device_id_type=MESH,
    )

    @pl.when((core == 0) & jnp.logical_not(lowest))
    def _():
        turn_bases(0)
        swap_rows.wait_recv()
        swap_right.wait_recv()
        joined[...] = dot(left_turned[0], right[1], NT).astype(jnp.bfloat16)
        swap_left.wait_recv()
        left_turned[1] = left[1].T

        def body(slot):
            pl.when(slot > 0)(lambda: count_lower(slot - 1))
            for part in range(2):
                forward_copy(slot, part, twin).wait_recv()
                lower_mix = scaled(dot(forward_in[slot, part], right_turned[0], NN), slot, 0)
                kept[part * half : (part + 1) * half] = lower_mix
                upper_mix = scaled(dot(lower_mix, joined[...], NN), slot, 1)
                fresh = dot(upper_mix, left_turned[1], NN).astype(jnp.bfloat16)
                forward_out[slot, part] = fresh
                pl.when(inner)(lambda: forward_copy(slot, part, spot + 2).start())
                count_in(fresh, slot, 1)

        each(body)

    def count_kept(slot):
        fresh = dot(kept[...], right[1], NN).astype(jnp.bfloat16)
        count_in(fresh, slot, 1)

    @pl.when((core == 1) & jnp.logical_not(highest))
    def _():
        swap_rows.wait_recv()
        swap_left.wait_recv()
        joined[...] = dot(right[1], left[0], NN).astype(jnp.bfloat16)
        swap_right.wait_recv()

        def body(slot):
            pl.when(slot > 0)(lambda: count_kept(slot - 1))
            for part in range(2):
                backward_copy(slot, part, twin).wait_recv()
                upper_mix = scaled(dot(backward_in[slot, part], left[1], NN), slot, 1)
                kept[part * half : (part + 1) * half] = upper_mix
                lower_mix = scaled(dot(upper_mix, joined[...], NN), slot, 0)
                fresh = dot(lower_mix, right[0], NN).astype(jnp.bfloat16)
                backward_out[slot, part] = fresh
                pl.when(inner)(lambda: backward_copy(slot, part, spot - 2).start())
                count_in(fresh, slot, 0)

        each(body)

    def share(side, step):
        return pltpu.make_async_remote_copy(
            src_ref=partial.at[side],
            dst_ref=gathered.at[team],
            send_sem=gather_send.at[side, step],
            recv_sem=gather_recv.at[step],
            device_id={"energy": lax.rem(team + step, teams), "slab": 2 * chip + side},
            device_id_type=MESH,
        )

    def speak(side):
        partial[side] = fold(side) + extra[side]
        for step in range(1, teams):
            share(side, step).start()
        pl.when(core != side)(share(side, 0).start)

        @pl.when(core == side)
        def _():
            gathered[team] = partial[side]

    pl.when((core == 0) & inner)(lambda: count_lower(count - 1))

    @pl.when(jnp.logical_not(speaks))
    def _():
        for side in range(2):
            mine[side] = fold(side)
        hand_over.start()

    @pl.when(speaks)
    def _():
        hand_over.wait_recv()

        @pl.when(highest)
        def _():
            speak(1)
            count_lower(count - 1)
            speak(0)

        @pl.when(jnp.logical_not(highest))
        def _():
            speak(0)
            count_kept(count - 1)
            speak(1)

    @pl.when(sends_forward | (spot == 0))
    def _():
        for part in range(2):
            each(lambda slot: forward_copy(slot, part, twin).wait_send())

    @pl.when(sends_backward | (spot == chain - 1))
    def _():
        for part in range(2):
            each(lambda slot: backward_copy(slot, part, twin).wait_send())

    @pl.when(inner | (spot == 0) | (spot == chain - 1))
    def _():
        swap_rows.wait_send()
        swap_right.wait_send()
        swap_left.wait_send()

    pl.when(jnp.logical_not(speaks))(hand_over.wait_send)

    @pl.when(speaks)
    def _():
        for side in range(2):
            for step in range(1, teams):
                share(side, step).wait_send()
            pl.when(core != side)(share(side, 0).wait_send)

    pl.when(jnp.logical_not(speaks))(share(0, 0).wait_recv)
    for step in range(1, teams):
        share(0, step).wait_recv()
    total = gathered[0]
    for member in range(1, teams):
        total += gathered[member]
    out[...] = total


def local(
    teams,
    chain,
    left_basis,
    right_basis,
    potential_index,
    levels,
    energy_values,
    energy_weights,
    energy_index,
    left_source,
    right_source,
):
    count = energy_index.shape[0]
    orbitals = left_basis.shape[1]
    modes = left_source.shape[1]
    outside = pl.BlockSpec(memory_space=pltpu.HBM)
    square = pltpu.VMEM((2, orbitals, orbitals), jnp.bfloat16)
    block = pltpu.VMEM((count, 2, modes // 2, orbitals), jnp.bfloat16)
    copies = pltpu.SemaphoreType.DMA((count, 2))
    pair = pltpu.VMEM((2, 1, orbitals), jnp.float32)
    return pl.pallas_call(
        functools.partial(kernel, chain, teams),
        out_shape=jax.ShapeDtypeStruct((1, orbitals), jnp.float32),
        in_specs=[outside] * 9,
        out_specs=pl.BlockSpec(memory_space=pltpu.VMEM),
        scratch_shapes=[
            pltpu.SMEM(potential_index.shape, jnp.int32),
            pltpu.SMEM(energy_values.shape, jnp.float32),
            pltpu.SMEM(energy_weights.shape, jnp.float32),
            pltpu.SMEM(energy_index.shape, jnp.int32),
            pltpu.VMEM(levels.shape, jnp.float32),
            pltpu.VMEM(left_source.shape, jnp.bfloat16),
            square,
            square,
            square,
            square,
            pltpu.VMEM((orbitals, orbitals), jnp.bfloat16),
            pltpu.VMEM((2, 1, orbitals), jnp.float32),
            pltpu.VMEM((modes, orbitals), jnp.float32),
            pltpu.VMEM((modes, orbitals), jnp.bfloat16),
            pltpu.VMEM((2, 8, orbitals), jnp.float32),
            pair,
            pair,
            pair,
            pltpu.VMEM((teams, 1, orbitals), jnp.float32),
            block,
            block,
            block,
            block,
            pltpu.SemaphoreType.DMA((8,)),
            pltpu.SemaphoreType.DMA((3,)),
            pltpu.SemaphoreType.DMA((3,)),
            copies,
            copies,
            copies,
            copies,
            pltpu.SemaphoreType.DMA((1,)),
            pltpu.SemaphoreType.DMA((1,)),
            pltpu.SemaphoreType.DMA((2, teams)),
            pltpu.SemaphoreType.DMA((teams,)),
        ],
        compiler_params=pltpu.CompilerParams(
            collective_id=0, has_side_effects=True, vmem_limit_bytes=63 << 20
        ),
    )(
        potential_index,
        energy_values,
        energy_weights,
        energy_index,
        levels,
        left_source,
        right_source,
        left_basis,
        right_basis,
    )


def solution(mesh):
    placed = (
        P("slab", None, None),
        P("slab", None, None),
        P("slab"),
        P(),
        P(),
        P(),
        P("energy"),
        P(),
        P(),
    )
    return jax.shard_map(
        functools.partial(local, mesh.shape["energy"], mesh.shape["slab"]),
        mesh=mesh,
        in_specs=placed,
        out_specs=P("slab", None),
        check_vma=False,
    )
```

```python
import functools

import jax
import jax.numpy as jnp
from jax import lax
from jax.experimental import pallas as pl
from jax.experimental.pallas import tpu as pltpu
from jax.sharding import PartitionSpec as P

MESH = pl.DeviceIdType.MESH
NN = (((1,), (0,)), ((), ()))
NT = (((1,), (1,)), ((), ()))


def dot(a, b, dims):
    return lax.dot_general(a, b, dims, preferred_element_type=jnp.float32)


def kernel(
    chain,
    teams,
    potential,
    energies_hbm,
    weights_hbm,
    indices_hbm,
    levels_hbm,
    left_source_hbm,
    right_source_hbm,
    left_hbm,
    right_hbm,
    out,
    energies,
    weights,
    indices,
    levels,
    source,
    left,
    right,
    left_turned,
    right_turned,
    joined,
    rows,
    first,
    kept,
    density,
    mine,
    extra,
    partial,
    gathered,
    forward_in,
    forward_out,
    backward_in,
    backward_out,
    load_sem,
    swap_send,
    swap_recv,
    forward_send,
    forward_recv,
    backward_send,
    backward_recv,
    extra_send,
    extra_recv,
    gather_send,
    gather_recv,
):
    count = indices.shape[0]
    modes = source.shape[1]
    orbitals = levels.shape[1]
    half = modes // 2
    spot = lax.axis_index("slab")
    team = lax.axis_index("energy")
    chips = chain // 2
    chip = spot // 2
    core = spot % 2
    twin = spot + 1 - 2 * core
    lowest = chip == 0
    highest = chip == chips - 1
    inner = jnp.logical_not(lowest | highest)
    upper = chip >= chips // 2
    speaker = jnp.where(highest, 0, 1)
    speaks = core == speaker

    def load(origin, target, place):
        return pltpu.make_async_copy(origin, target, load_sem.at[place])

    left_load = load(left_source_hbm, source, 0)
    right_load = load(right_source_hbm, source, 0)
    right_base = load(right_hbm.at[0], right.at[core], 1)
    left_base = load(left_hbm.at[0], left.at[core], 2)
    tables = [
        load(energies_hbm, energies, 3),
        load(weights_hbm, weights, 4),
        load(indices_hbm, indices, 5),
        load(levels_hbm, levels, 6),
    ]
    pl.when(spot == 0)(left_load.start)
    pl.when(spot == chain - 1)(right_load.start)
    left_base.start()
    for item in tables:
        item.start()
    right_base.start()

    barrier = pltpu.get_barrier_semaphore()

    def greet(place):
        pl.semaphore_signal(barrier, inc=1, device_id=place, device_id_type=MESH)

    greet({"slab": twin})
    pl.when((core == 0) & jnp.logical_not(lowest))(
        lambda: greet({"slab": jnp.where(chip == 1, 1, spot - 2)})
    )
    pl.when((core == 1) & jnp.logical_not(highest))(
        lambda: greet({"slab": jnp.where(chip == chips - 2, chain - 2, spot + 2)})
    )
    for step in range(1, teams):
        greet({"energy": lax.rem(team + step, teams), "slab": 2 * chip + speaker})
    sends_forward = jnp.where(lowest, core == 1, (core == 0) & jnp.logical_not(highest))
    sends_backward = jnp.where(highest, core == 0, (core == 1) & jnp.logical_not(lowest))
    greetings = (
        1
        + sends_forward.astype(jnp.int32)
        + sends_backward.astype(jnp.int32)
        + jnp.where(speaks, 2 * (teams - 1), 0)
    )

    density[...] = jnp.zeros_like(density)
    for item in tables:
        item.wait()
    rows[core] = levels[pl.ds(potential[0], 1), :]

    def swap(origin, target, place):
        return pltpu.make_async_remote_copy(
            src_ref=origin,
            dst_ref=target,
            send_sem=swap_send.at[place],
            recv_sem=swap_recv.at[place],
            device_id={"slab": twin},
            device_id_type=MESH,
        )

    swap_rows = swap(rows.at[core], rows.at[core], 0)
    swap_right = swap(right_hbm.at[0], right.at[core], 1)
    swap_left = swap(left_hbm.at[0], left.at[core], 2)

    def start_swaps():
        swap_rows.start()

        @pl.when(core == 0)
        def _():
            swap_left.start()
            swap_right.start()

        @pl.when(core == 1)
        def _():
            swap_right.start()
            swap_left.start()

    def settle_bases():
        right_base.wait()
        left_base.wait()

    def turned_source():
        return source[...].astype(jnp.float32).T.astype(jnp.bfloat16)

    def turn_bases(side):
        left_turned[side] = left[side].T
        right_turned[side] = right[side].T

    @pl.when(spot == 0)
    def _():
        settle_bases()
        left_load.wait()
        first[...] = dot(turned_source(), right[0], NT)

    @pl.when(spot == chain - 1)
    def _():
        right_load.wait()
        left_base.wait()
        first[...] = dot(turned_source(), left[1], NN)
        right_base.wait()

    @pl.when(spot == 1)
    def _():
        settle_bases()
        turn_bases(1)

    pl.when(spot == chain - 2)(settle_bases)
    pl.semaphore_wait(barrier, greetings)

    @pl.when(inner)
    def _():
        start_swaps()
        settle_bases()

    def forward_copy(slot, part, place):
        return pltpu.make_async_remote_copy(
            src_ref=forward_out.at[slot, part],
            dst_ref=forward_in.at[slot, part],
            send_sem=forward_send.at[slot, part],
            recv_sem=forward_recv.at[slot, part],
            device_id={"slab": place},
            device_id_type=MESH,
        )

    def backward_copy(slot, part, place):
        return pltpu.make_async_remote_copy(
            src_ref=backward_out.at[slot, part],
            dst_ref=backward_in.at[slot, part],
            send_sem=backward_send.at[slot, part],
            recv_sem=backward_recv.at[slot, part],
            device_id={"slab": place},
            device_id_type=MESH,
        )

    def scaled(mixed, slot, side):
        scale = 1.0 / (energies[indices[slot]] - rows[side])
        return (scale * mixed).astype(jnp.bfloat16)

    def count_in(state, slot, side):
        weight = weights[indices[slot]] / (count * teams * modes)
        squared = state.astype(jnp.float32) ** 2
        part = jnp.sum(squared.reshape(-1, 8, orbitals), axis=0)
        density[side] += weight * part

    def down(state, slot, side):
        mixed = dot(state, right_turned[side], NN)
        return dot(scaled(mixed, slot, side), left_turned[side], NN).astype(jnp.bfloat16)

    def up(state, slot, side):
        mixed = dot(state, left[side], NN)
        return dot(scaled(mixed, slot, side), right[side], NN).astype(jnp.bfloat16)

    def each(body):
        def step(slot, carry):
            body(slot)
            return carry

        lax.fori_loop(0, count, step, 0)

    @pl.when(spot == 0)
    def _():
        def body(slot):
            fresh = dot(scaled(first[...], slot, 0), left[0], NT).astype(jnp.bfloat16)
            for part in range(2):
                forward_out[slot, part] = fresh[part * half : (part + 1) * half]
                forward_copy(slot, part, twin).start()
            count_in(fresh, slot, 0)

        each(body)
        start_swaps()

    @pl.when(spot == 1)
    def _():
        def body(slot):
            for part in range(2):
                forward_copy(slot, part, twin).wait_recv()
                fresh = down(forward_in[slot, part], slot, 1)
                forward_out[slot, part] = fresh
                forward_copy(slot, part, 2).start()
                count_in(fresh, slot, 1)

        each(body)

    @pl.when(spot == chain - 1)
    def _():
        def body(slot):
            fresh = dot(scaled(first[...], slot, 1), right[1], NN).astype(jnp.bfloat16)
            for part in range(2):
                backward_out[slot, part] = fresh[part * half : (part + 1) * half]
                backward_copy(slot, part, twin).start()
            count_in(fresh, slot, 1)

        each(body)
        start_swaps()

    @pl.when(spot == chain - 2)
    def _():
        def body(slot):
            for part in range(2):
                backward_copy(slot, part, twin).wait_recv()
                fresh = up(backward_in[slot, part], slot, 0)
                backward_out[slot, part] = fresh
                backward_copy(slot, part, chain - 3).start()
                count_in(fresh, slot, 0)

        each(body)

    def count_lower(slot):
        fresh = dot(kept[...], left_turned[0], NN).astype(jnp.bfloat16)
        count_in(fresh, slot, 0)

    def fold(side):
        return jnp.sum(density[side], axis=0, keepdims=True)

    hand_over = pltpu.make_async_remote_copy(
        src_ref=mine,
        dst_ref=extra,
        send_sem=extra_send.at[0],
        recv_sem=extra_recv.at[0],
        device_id={"slab": twin},
        device_id_type=MESH,
    )

    @pl.when((core == 0) & jnp.logical_not(lowest))
    def _():
        turn_bases(0)
        swap_rows.wait_recv()
        swap_right.wait_recv()
        joined[...] = dot(left_turned[0], right[1], NT).astype(jnp.bfloat16)
        swap_left.wait_recv()
        left_turned[1] = left[1].T

        def body(slot):
            pl.when(slot > 0)(lambda: count_lower(slot - 1))
            for part in range(2):
                forward_copy(slot, part, twin).wait_recv()
                lower_mix = scaled(dot(forward_in[slot, part], right_turned[0], NN), slot, 0)
                kept[part * half : (part + 1) * half] = lower_mix
                upper_mix = scaled(dot(lower_mix, joined[...], NN), slot, 1)
                fresh = dot(upper_mix, left_turned[1], NN).astype(jnp.bfloat16)
                forward_out[slot, part] = fresh
                pl.when(inner)(lambda: forward_copy(slot, part, spot + 2).start())
                count_in(fresh, slot, 1)

        each(body)

    def count_kept(slot):
        fresh = dot(kept[...], right[1], NN).astype(jnp.bfloat16)
        count_in(fresh, slot, 1)

    @pl.when((core == 1) & jnp.logical_not(highest))
    def _():
        swap_rows.wait_recv()
        swap_left.wait_recv()
        joined[...] = dot(right[1], left[0], NN).astype(jnp.bfloat16)
        swap_right.wait_recv()

        def body(slot):
            pl.when(slot > 0)(lambda: count_kept(slot - 1))
            for part in range(2):
                backward_copy(slot, part, twin).wait_recv()
                upper_mix = scaled(dot(backward_in[slot, part], left[1], NN), slot, 1)
                kept[part * half : (part + 1) * half] = upper_mix
                lower_mix = scaled(dot(upper_mix, joined[...], NN), slot, 0)
                fresh = dot(lower_mix, right[0], NN).astype(jnp.bfloat16)
                backward_out[slot, part] = fresh
                pl.when(inner)(lambda: backward_copy(slot, part, spot - 2).start())
                count_in(fresh, slot, 0)

        each(body)

    def share(side, step):
        return pltpu.make_async_remote_copy(
            src_ref=partial.at[side],
            dst_ref=gathered.at[team],
            send_sem=gather_send.at[side, step],
            recv_sem=gather_recv.at[step],
            device_id={"energy": lax.rem(team + step, teams), "slab": 2 * chip + side},
            device_id_type=MESH,
        )

    def speak(side):
        partial[side] = fold(side) + extra[side]
        for step in range(1, teams):
            share(side, step).start()
        pl.when(core != side)(share(side, 0).start)

        @pl.when(core == side)
        def _():
            gathered[team] = partial[side]

    pl.when((core == 0) & inner)(lambda: count_lower(count - 1))

    @pl.when(jnp.logical_not(speaks))
    def _():
        for side in range(2):
            mine[side] = fold(side)
        hand_over.start()

    @pl.when(speaks)
    def _():
        hand_over.wait_recv()

        @pl.when(highest)
        def _():
            speak(1)
            count_lower(count - 1)
            speak(0)

        @pl.when(jnp.logical_not(highest))
        def _():
            speak(0)
            count_kept(count - 1)
            speak(1)

    @pl.when(sends_forward | (spot == 0))
    def _():
        for part in range(2):
            each(lambda slot: forward_copy(slot, part, twin).wait_send())

    @pl.when(sends_backward | (spot == chain - 1))
    def _():
        for part in range(2):
            each(lambda slot: backward_copy(slot, part, twin).wait_send())

    @pl.when(inner | (spot == 0) | (spot == chain - 1))
    def _():
        swap_rows.wait_send()
        swap_right.wait_send()
        swap_left.wait_send()

    pl.when(jnp.logical_not(speaks))(hand_over.wait_send)

    @pl.when(speaks)
    def _():
        for side in range(2):
            for step in range(1, teams):
                share(side, step).wait_send()
            pl.when(core != side)(share(side, 0).wait_send)

    pl.when(jnp.logical_not(speaks))(share(0, 0).wait_recv)
    for step in range(1, teams):
        share(0, step).wait_recv()
    total = gathered[0]
    for member in range(1, teams):
        total += gathered[member]
    out[...] = total


def local(
    teams,
    chain,
    left_basis,
    right_basis,
    potential_index,
    levels,
    energy_values,
    energy_weights,
    energy_index,
    left_source,
    right_source,
):
    count = energy_index.shape[0]
    orbitals = left_basis.shape[1]
    modes = left_source.shape[1]
    outside = pl.BlockSpec(memory_space=pltpu.HBM)
    square = pltpu.VMEM((2, orbitals, orbitals), jnp.bfloat16)
    block = pltpu.VMEM((count, 2, modes // 2, orbitals), jnp.bfloat16)
    copies = pltpu.SemaphoreType.DMA((count, 2))
    pair = pltpu.VMEM((2, 1, orbitals), jnp.float32)
    return pl.pallas_call(
        functools.partial(kernel, chain, teams),
        out_shape=pltpu.VMEM((1, orbitals), jnp.float32),
        in_specs=[pl.BlockSpec(memory_space=pltpu.SMEM)] + [outside] * 8,
        out_specs=pl.BlockSpec(memory_space=pltpu.VMEM),
        scratch_shapes=[
            pltpu.SMEM(energy_values.shape, jnp.float32),
            pltpu.SMEM(energy_weights.shape, jnp.float32),
            pltpu.SMEM(energy_index.shape, jnp.int32),
            pltpu.VMEM(levels.shape, jnp.float32),
            pltpu.VMEM(left_source.shape, jnp.bfloat16),
            square,
            square,
            square,
            square,
            pltpu.VMEM((orbitals, orbitals), jnp.bfloat16),
            pltpu.VMEM((2, 1, orbitals), jnp.float32),
            pltpu.VMEM((modes, orbitals), jnp.float32),
            pltpu.VMEM((modes, orbitals), jnp.bfloat16),
            pltpu.VMEM((2, 8, orbitals), jnp.float32),
            pair,
            pair,
            pair,
            pltpu.VMEM((teams, 1, orbitals), jnp.float32),
            block,
            block,
            block,
            block,
            pltpu.SemaphoreType.DMA((7,)),
            pltpu.SemaphoreType.DMA((3,)),
            pltpu.SemaphoreType.DMA((3,)),
            copies,
            copies,
            copies,
            copies,
            pltpu.SemaphoreType.DMA((1,)),
            pltpu.SemaphoreType.DMA((1,)),
            pltpu.SemaphoreType.DMA((2, teams)),
            pltpu.SemaphoreType.DMA((teams,)),
        ],
        compiler_params=pltpu.CompilerParams(
            collective_id=0, has_side_effects=True, vmem_limit_bytes=63 << 20
        ),
    )(
        potential_index,
        energy_values,
        energy_weights,
        energy_index,
        levels,
        left_source,
        right_source,
        left_basis,
        right_basis,
    )


def solution(mesh):
    placed = (
        P("slab", None, None),
        P("slab", None, None),
        P("slab"),
        P(),
        P(),
        P(),
        P("energy"),
        P(),
        P(),
    )
    return jax.shard_map(
        functools.partial(local, mesh.shape["energy"], mesh.shape["slab"]),
        mesh=mesh,
        in_specs=placed,
        out_specs=P("slab", None),
        check_vma=False,
    )
```

```python
import functools

import jax
import jax.numpy as jnp
from jax import lax
from jax.experimental import pallas as pl
from jax.experimental.pallas import tpu as pltpu
from jax.sharding import PartitionSpec as P

MESH = pl.DeviceIdType.MESH
NN = (((1,), (0,)), ((), ()))
NT = (((1,), (1,)), ((), ()))


def dot(a, b, dims):
    return lax.dot_general(a, b, dims, preferred_element_type=jnp.float32)


def kernel(
    chain,
    teams,
    potential,
    energies_hbm,
    weights_hbm,
    indices_hbm,
    levels_hbm,
    left_source_hbm,
    right_source_hbm,
    left_hbm,
    right_hbm,
    out,
    energies,
    weights,
    indices,
    levels,
    source,
    left,
    right,
    left_turned,
    right_turned,
    joined,
    grid,
    rows,
    first,
    kept,
    density,
    mine,
    extra,
    partial,
    gathered,
    forward_in,
    forward_out,
    backward_in,
    backward_out,
    load_sem,
    gift_sem,
    swap_send,
    swap_recv,
    forward_send,
    forward_recv,
    backward_send,
    backward_recv,
    extra_send,
    extra_recv,
    gather_send,
    gather_recv,
):
    count = indices.shape[0]
    modes = source.shape[1]
    orbitals = levels.shape[1]
    half = modes // 2
    spot = lax.axis_index("slab")
    team = lax.axis_index("energy")
    chips = chain // 2
    chip = spot // 2
    core = spot % 2
    twin = spot + 1 - 2 * core
    lowest = chip == 0
    highest = chip == chips - 1
    inner = jnp.logical_not(lowest | highest)
    upper = chip >= chips // 2
    speaker = jnp.where(highest, 0, 1)
    speaks = core == speaker
    gives = (team == teams - 1) & (teams > 1)
    takes = (team == 0) & (teams > 1)
    slots = count + takes.astype(jnp.int32)
    whole = count - gives.astype(jnp.int32)

    def load(origin, target, place):
        return pltpu.make_async_copy(origin, target, load_sem.at[place])

    left_load = load(left_source_hbm, source, 0)
    right_load = load(right_source_hbm, source, 0)
    right_base = load(right_hbm.at[0], right.at[core], 1)
    left_base = load(left_hbm.at[0], left.at[core], 2)
    tables = [
        load(energies_hbm, energies, 3),
        load(weights_hbm, weights, 4),
        load(indices_hbm, indices, 5),
        load(levels_hbm, levels, 6),
    ]
    pl.when(spot == 0)(left_load.start)
    pl.when(spot == chain - 1)(right_load.start)
    left_base.start()
    for item in tables:
        item.start()
    right_base.start()

    barrier = pltpu.get_barrier_semaphore()

    def greet(place):
        pl.semaphore_signal(barrier, inc=1, device_id=place, device_id_type=MESH)

    greet({"slab": twin})
    pl.when((core == 0) & jnp.logical_not(lowest))(
        lambda: greet({"slab": jnp.where(chip == 1, 1, spot - 2)})
    )
    pl.when((core == 1) & jnp.logical_not(highest))(
        lambda: greet({"slab": jnp.where(chip == chips - 2, chain - 2, spot + 2)})
    )
    for step in range(1, teams):
        greet({"energy": lax.rem(team + step, teams), "slab": 2 * chip + speaker})
    pl.when(takes & jnp.logical_not(speaks))(lambda: greet({"energy": teams - 1}))
    sends_forward = jnp.where(lowest, core == 1, (core == 0) & jnp.logical_not(highest))
    sends_backward = jnp.where(highest, core == 0, (core == 1) & jnp.logical_not(lowest))
    greetings = (
        1
        + sends_forward.astype(jnp.int32)
        + sends_backward.astype(jnp.int32)
        + jnp.where(speaks, 2 * (teams - 1), gives.astype(jnp.int32))
    )

    density[...] = jnp.zeros_like(density)
    for item in tables:
        item.wait()
    rows[core] = levels[pl.ds(potential[0], 1), :]
    for slot in range(count):
        grid[slot, 0:1] = jnp.full((1, orbitals), energies[indices[slot]], jnp.float32)
        weight = weights[indices[slot]] / (count * teams * modes)
        grid[slot, 1:2] = jnp.full((1, orbitals), weight, jnp.float32)

    gift = pltpu.make_async_remote_copy(
        src_ref=grid.at[count - 1],
        dst_ref=grid.at[count],
        send_sem=gift_sem.at[0],
        recv_sem=gift_sem.at[1],
        device_id={"energy": 0},
        device_id_type=MESH,
    )

    def swap(origin, target, place):
        return pltpu.make_async_remote_copy(
            src_ref=origin,
            dst_ref=target,
            send_sem=swap_send.at[place],
            recv_sem=swap_recv.at[place],
            device_id={"slab": twin},
            device_id_type=MESH,
        )

    swap_rows = swap(rows.at[core], rows.at[core], 0)
    swap_right = swap(right_hbm.at[0], right.at[core], 1)
    swap_left = swap(left_hbm.at[0], left.at[core], 2)

    def start_swaps():
        swap_rows.start()

        @pl.when(core == 0)
        def _():
            swap_left.start()
            swap_right.start()

        @pl.when(core == 1)
        def _():
            swap_right.start()
            swap_left.start()

    def settle_bases():
        right_base.wait()
        left_base.wait()

    def turned_source():
        return source[...].astype(jnp.float32).T.astype(jnp.bfloat16)

    def turn_bases(side):
        left_turned[side] = left[side].T
        right_turned[side] = right[side].T

    @pl.when(spot == 0)
    def _():
        settle_bases()
        left_load.wait()
        first[...] = dot(turned_source(), right[0], NT)

    @pl.when(spot == chain - 1)
    def _():
        right_load.wait()
        left_base.wait()
        first[...] = dot(turned_source(), left[1], NN)
        right_base.wait()

    @pl.when(spot == 1)
    def _():
        settle_bases()
        turn_bases(1)

    pl.when(spot == chain - 2)(settle_bases)
    pl.semaphore_wait(barrier, greetings)
    pl.when(gives)(gift.start)

    @pl.when(inner)
    def _():
        start_swaps()
        settle_bases()

    def forward_copy(slot, part, place):
        return pltpu.make_async_remote_copy(
            src_ref=forward_out.at[slot, part],
            dst_ref=forward_in.at[slot, part],
            send_sem=forward_send.at[slot, part],
            recv_sem=forward_recv.at[slot, part],
            device_id={"slab": place},
            device_id_type=MESH,
        )

    def backward_copy(slot, part, place):
        return pltpu.make_async_remote_copy(
            src_ref=backward_out.at[slot, part],
            dst_ref=backward_in.at[slot, part],
            send_sem=backward_send.at[slot, part],
            recv_sem=backward_recv.at[slot, part],
            device_id={"slab": place},
            device_id_type=MESH,
        )

    def scaled(mixed, slot, side):
        scale = 1.0 / (grid[slot, 0:1] - rows[side])
        return (scale * mixed).astype(jnp.bfloat16)

    def count_in(state, slot, side):
        squared = state.astype(jnp.float32) ** 2
        part = jnp.sum(squared.reshape(-1, 8, orbitals), axis=0)
        density[side] += grid[slot, 1:2] * part

    def down(state, slot, side):
        mixed = dot(state, right_turned[side], NN)
        return dot(scaled(mixed, slot, side), left_turned[side], NN).astype(jnp.bfloat16)

    def up(state, slot, side):
        mixed = dot(state, left[side], NN)
        return dot(scaled(mixed, slot, side), right[side], NN).astype(jnp.bfloat16)

    def each(body):
        def step(slot, carry):
            body(slot)
            return carry

        lax.fori_loop(0, slots, step, 0)

    def parts(slot, body, order=(0, 1)):
        for part in order:
            if part:
                pl.when(slot < whole)(functools.partial(body, part))
            else:
                body(part)

    def near_end(side, refs, copy, close):
        def body(slot):
            pl.when(slot == count)(gift.wait_recv)
            fresh = close(scaled(first[...], slot, side)).astype(jnp.bfloat16)

            head = jnp.where(slot == count, fresh[half:], fresh[:half])
            pieces = (head, fresh[half:])

            def send(part):
                refs[slot, part] = pieces[part]
                copy(slot, part, twin).start()

            parts(slot, send)
            parts(slot, lambda part: count_in(pieces[part], slot, side))

        each(body)
        start_swaps()

    def far_end(side, given, refs, copy, advance, place):
        def body(slot):
            pl.when(slot == count)(gift.wait_recv)

            def pass_on(part):
                copy(slot, part, twin).wait_recv()
                fresh = advance(given[slot, part], slot, side)
                refs[slot, part] = fresh
                copy(slot, part, place).start()
                count_in(fresh, slot, side)

            parts(slot, pass_on)

        each(body)

    @pl.when(spot == 0)
    def _():
        near_end(0, forward_out, forward_copy, lambda mixed: dot(mixed, left[0], NT))

    @pl.when(spot == 1)
    def _():
        far_end(1, forward_in, forward_out, forward_copy, down, 2)

    @pl.when(spot == chain - 1)
    def _():
        near_end(1, backward_out, backward_copy, lambda mixed: dot(mixed, right[1], NN))

    @pl.when(spot == chain - 2)
    def _():
        far_end(0, backward_in, backward_out, backward_copy, up, chain - 3)

    def sweep(given, refs, copy, bases, near, onward, count_rest):
        entry, link, exit_ = bases
        far = 1 - near

        def body(slot):
            pl.when(slot > 0)(lambda: count_rest(slot - 1))
            pl.when((slot == count) & inner)(gift.wait_recv)

            @pl.when(slot >= whole)
            def _():
                kept[half:] = jnp.zeros((half, orbitals), jnp.bfloat16)

            def advance(part):
                copy(slot, part, twin).wait_recv()
                near_mix = scaled(dot(given[slot, part], entry[...], NN), slot, near)
                kept[part * half : (part + 1) * half] = near_mix
                far_mix = scaled(dot(near_mix, link[...], NN), slot, far)
                fresh = dot(far_mix, exit_[...], NN).astype(jnp.bfloat16)
                refs[slot, part] = fresh
                pl.when(inner)(lambda: copy(slot, part, onward).start())
                count_in(fresh, slot, far)

            parts(slot, advance)

        each(body)

    def count_lower(slot):
        fresh = dot(kept[...], left_turned[0], NN).astype(jnp.bfloat16)
        count_in(fresh, slot, 0)

    def count_upper(slot):
        fresh = dot(kept[...], right[1], NN).astype(jnp.bfloat16)
        count_in(fresh, slot, 1)

    @pl.when((core == 0) & jnp.logical_not(lowest))
    def _():
        turn_bases(0)
        swap_rows.wait_recv()
        swap_right.wait_recv()
        joined[...] = dot(left_turned[0], right[1], NT).astype(jnp.bfloat16)
        swap_left.wait_recv()
        left_turned[1] = left[1].T
        sweep(
            forward_in, forward_out, forward_copy,
            (right_turned.at[0], joined, left_turned.at[1]), 0, spot + 2, count_lower,
        )

    @pl.when((core == 1) & jnp.logical_not(highest))
    def _():
        swap_rows.wait_recv()
        swap_left.wait_recv()
        joined[...] = dot(right[1], left[0], NN).astype(jnp.bfloat16)
        swap_right.wait_recv()
        sweep(
            backward_in, backward_out, backward_copy,
            (left.at[1], joined, right.at[0]), 1, spot - 2, count_upper,
        )

    def fold(side):
        return jnp.sum(density[side], axis=0, keepdims=True)

    hand_over = pltpu.make_async_remote_copy(
        src_ref=mine,
        dst_ref=extra,
        send_sem=extra_send.at[0],
        recv_sem=extra_recv.at[0],
        device_id={"slab": twin},
        device_id_type=MESH,
    )

    def share(side, step):
        return pltpu.make_async_remote_copy(
            src_ref=partial.at[side],
            dst_ref=gathered.at[team],
            send_sem=gather_send.at[side, step],
            recv_sem=gather_recv.at[step],
            device_id={"energy": lax.rem(team + step, teams), "slab": 2 * chip + side},
            device_id_type=MESH,
        )

    def speak(side):
        partial[side] = fold(side) + extra[side]
        for step in range(1, teams):
            share(side, step).start()
        pl.when(core != side)(share(side, 0).start)

        @pl.when(core == side)
        def _():
            gathered[team] = partial[side]

    pl.when((core == 0) & inner)(lambda: count_lower(slots - 1))

    @pl.when(jnp.logical_not(speaks))
    def _():
        for side in range(2):
            mine[side] = fold(side)
        hand_over.start()

    @pl.when(speaks)
    def _():
        hand_over.wait_recv()

        @pl.when(highest)
        def _():
            speak(1)
            count_lower(slots - 1)
            speak(0)

        @pl.when(jnp.logical_not(highest))
        def _():
            speak(0)
            count_upper(slots - 1)
            speak(1)

    @pl.when(sends_forward | (spot == 0))
    def _():
        each(lambda slot: parts(slot, lambda part: forward_copy(slot, part, twin).wait_send()))

    @pl.when(sends_backward | (spot == chain - 1))
    def _():
        each(lambda slot: parts(slot, lambda part: backward_copy(slot, part, twin).wait_send()))

    @pl.when(inner | (spot == 0) | (spot == chain - 1))
    def _():
        swap_rows.wait_send()
        swap_right.wait_send()
        swap_left.wait_send()

    pl.when(jnp.logical_not(speaks))(hand_over.wait_send)
    pl.when(gives)(gift.wait_send)

    @pl.when(speaks)
    def _():
        for side in range(2):
            for step in range(1, teams):
                share(side, step).wait_send()
            pl.when(core != side)(share(side, 0).wait_send)

    pl.when(jnp.logical_not(speaks))(share(0, 0).wait_recv)
    for step in range(1, teams):
        share(0, step).wait_recv()
    total = gathered[0]
    for member in range(1, teams):
        total += gathered[member]
    out[...] = total


def local(
    teams,
    chain,
    left_basis,
    right_basis,
    potential_index,
    levels,
    energy_values,
    energy_weights,
    energy_index,
    left_source,
    right_source,
):
    count = energy_index.shape[0]
    orbitals = left_basis.shape[1]
    modes = left_source.shape[1]
    outside = pl.BlockSpec(memory_space=pltpu.HBM)
    square = pltpu.VMEM((2, orbitals, orbitals), jnp.bfloat16)
    block = pltpu.VMEM((count + 1, 2, modes // 2, orbitals), jnp.bfloat16)
    copies = pltpu.SemaphoreType.DMA((count + 1, 2))
    pair = pltpu.VMEM((2, 1, orbitals), jnp.float32)
    return pl.pallas_call(
        functools.partial(kernel, chain, teams),
        out_shape=pltpu.VMEM((1, orbitals), jnp.float32),
        in_specs=[pl.BlockSpec(memory_space=pltpu.SMEM)] + [outside] * 8,
        out_specs=pl.BlockSpec(memory_space=pltpu.VMEM),
        scratch_shapes=[
            pltpu.SMEM(energy_values.shape, jnp.float32),
            pltpu.SMEM(energy_weights.shape, jnp.float32),
            pltpu.SMEM(energy_index.shape, jnp.int32),
            pltpu.VMEM(levels.shape, jnp.float32),
            pltpu.VMEM(left_source.shape, jnp.bfloat16),
            square,
            square,
            square,
            square,
            pltpu.VMEM((orbitals, orbitals), jnp.bfloat16),
            pltpu.VMEM((count + 1, 2, orbitals), jnp.float32),
            pltpu.VMEM((2, 1, orbitals), jnp.float32),
            pltpu.VMEM((modes, orbitals), jnp.float32),
            pltpu.VMEM((modes, orbitals), jnp.bfloat16),
            pltpu.VMEM((2, 8, orbitals), jnp.float32),
            pair,
            pair,
            pair,
            pltpu.VMEM((teams, 1, orbitals), jnp.float32),
            block,
            block,
            block,
            block,
            pltpu.SemaphoreType.DMA((7,)),
            pltpu.SemaphoreType.DMA((2,)),
            pltpu.SemaphoreType.DMA((3,)),
            pltpu.SemaphoreType.DMA((3,)),
            copies,
            copies,
            copies,
            copies,
            pltpu.SemaphoreType.DMA((1,)),
            pltpu.SemaphoreType.DMA((1,)),
            pltpu.SemaphoreType.DMA((2, teams)),
            pltpu.SemaphoreType.DMA((teams,)),
        ],
        compiler_params=pltpu.CompilerParams(
            collective_id=0, has_side_effects=True, vmem_limit_bytes=63 << 20
        ),
    )(
        potential_index,
        energy_values,
        energy_weights,
        energy_index,
        levels,
        left_source,
        right_source,
        left_basis,
        right_basis,
    )


def solution(mesh):
    placed = (
        P("slab", None, None),
        P("slab", None, None),
        P("slab"),
        P(),
        P(),
        P(),
        P("energy"),
        P(),
        P(),
    )
    return jax.shard_map(
        functools.partial(local, mesh.shape["energy"], mesh.shape["slab"]),
        mesh=mesh,
        in_specs=placed,
        out_specs=P("slab", None),
        check_vma=False,
    )
```

```python
import functools

import jax
import jax.numpy as jnp
from jax import lax
from jax.experimental import pallas as pl
from jax.experimental.pallas import tpu as pltpu
from jax.sharding import PartitionSpec as P

MESH = pl.DeviceIdType.MESH
NN = (((1,), (0,)), ((), ()))
NT = (((1,), (1,)), ((), ()))


def dot(a, b, dims):
    return lax.dot_general(a, b, dims, preferred_element_type=jnp.float32)


def kernel(
    chain,
    teams,
    potential,
    energies_hbm,
    weights_hbm,
    indices_hbm,
    levels_hbm,
    left_source_hbm,
    right_source_hbm,
    left_hbm,
    right_hbm,
    out,
    energies,
    weights,
    indices,
    levels,
    source,
    left,
    right,
    left_turned,
    right_turned,
    joined,
    grid,
    rows,
    first,
    kept,
    density,
    mine,
    extra,
    partial,
    gathered,
    forward_in,
    forward_out,
    backward_in,
    backward_out,
    load_sem,
    gift_sem,
    swap_send,
    swap_recv,
    forward_send,
    forward_recv,
    backward_send,
    backward_recv,
    extra_sem,
    gather_send,
    gather_recv,
):
    count = indices.shape[0]
    modes = source.shape[1]
    orbitals = levels.shape[1]
    half = modes // 2
    spot = lax.axis_index("slab")
    team = lax.axis_index("energy")
    chips = chain // 2
    chip = spot // 2
    core = spot % 2
    twin = spot + 1 - 2 * core
    lowest = chip == 0
    highest = chip == chips - 1
    inner = jnp.logical_not(lowest | highest)
    upper = chip >= chips // 2
    speaker = jnp.where(highest, 0, 1)
    speaks = core == speaker
    gives = (team == teams - 1) & (teams > 1)
    takes = (team == 0) & (teams > 1)
    slots = count + takes.astype(jnp.int32)
    whole = count - gives.astype(jnp.int32)

    def load(origin, target, place):
        return pltpu.make_async_copy(origin, target, load_sem.at[place])

    left_load = load(left_source_hbm, source, 0)
    right_load = load(right_source_hbm, source, 0)
    right_base = load(right_hbm.at[0], right.at[core], 1)
    left_base = load(left_hbm.at[0], left.at[core], 2)
    tables = [
        load(energies_hbm, energies, 3),
        load(weights_hbm, weights, 4),
        load(indices_hbm, indices, 5),
        load(levels_hbm, levels, 6),
    ]
    pl.when(spot == 0)(left_load.start)
    pl.when(spot == chain - 1)(right_load.start)
    left_base.start()
    for item in tables:
        item.start()
    right_base.start()

    barrier = pltpu.get_barrier_semaphore()

    def greet(place):
        pl.semaphore_signal(barrier, inc=1, device_id=place, device_id_type=MESH)

    greet({"slab": twin})
    pl.when((core == 0) & jnp.logical_not(lowest))(
        lambda: greet({"slab": jnp.where(chip == 1, 1, spot - 2)})
    )
    pl.when((core == 1) & jnp.logical_not(highest))(
        lambda: greet({"slab": jnp.where(chip == chips - 2, chain - 2, spot + 2)})
    )
    for step in range(1, teams):
        greet({"energy": lax.rem(team + step, teams), "slab": 2 * chip + speaker})
    pl.when(takes & jnp.logical_not(speaks))(lambda: greet({"energy": teams - 1}))
    sends_forward = jnp.where(lowest, core == 1, (core == 0) & jnp.logical_not(highest))
    sends_backward = jnp.where(highest, core == 0, (core == 1) & jnp.logical_not(lowest))
    greetings = (
        1
        + sends_forward.astype(jnp.int32)
        + sends_backward.astype(jnp.int32)
        + jnp.where(speaks, 2 * (teams - 1), gives.astype(jnp.int32))
    )

    density[...] = jnp.zeros_like(density)
    for item in tables:
        item.wait()
    rows[core] = levels[pl.ds(potential[0], 1), :]
    for slot in range(count):
        grid[slot, 0:1] = jnp.full((1, orbitals), energies[indices[slot]], jnp.float32)
        weight = weights[indices[slot]] / (count * teams * modes)
        grid[slot, 1:2] = jnp.full((1, orbitals), weight, jnp.float32)

    gift = pltpu.make_async_remote_copy(
        src_ref=grid.at[count - 1],
        dst_ref=grid.at[count],
        send_sem=gift_sem.at[0],
        recv_sem=gift_sem.at[0],
        device_id={"energy": 0},
        device_id_type=MESH,
    )

    def swap(origin, target, place):
        return pltpu.make_async_remote_copy(
            src_ref=origin,
            dst_ref=target,
            send_sem=swap_send.at[min(place, 1)],
            recv_sem=swap_recv.at[place],
            device_id={"slab": twin},
            device_id_type=MESH,
        )

    swap_rows = swap(rows.at[core], rows.at[core], 0)
    swap_right = swap(right_hbm.at[0], right.at[core], 1)
    swap_left = swap(left_hbm.at[0], left.at[core], 2)

    def start_swaps():
        swap_rows.start()

        @pl.when(core == 0)
        def _():
            swap_left.start()
            swap_right.start()

        @pl.when(core == 1)
        def _():
            swap_right.start()
            swap_left.start()

    def settle_bases():
        right_base.wait()
        left_base.wait()

    def turned_source():
        return source[...].astype(jnp.float32).T.astype(jnp.bfloat16)

    def turn_bases(side):
        left_turned[side] = left[side].T
        right_turned[side] = right[side].T

    @pl.when(spot == 0)
    def _():
        settle_bases()
        left_load.wait()
        first[...] = dot(turned_source(), right[0], NT)

    @pl.when(spot == chain - 1)
    def _():
        right_load.wait()
        left_base.wait()
        first[...] = dot(turned_source(), left[1], NN)
        right_base.wait()

    @pl.when(spot == 1)
    def _():
        settle_bases()
        turn_bases(1)

    pl.when(spot == chain - 2)(settle_bases)
    pl.semaphore_wait(barrier, greetings)
    pl.when(gives)(gift.start)

    @pl.when(inner)
    def _():
        start_swaps()
        settle_bases()

    def forward_copy(slot, part, place):
        return pltpu.make_async_remote_copy(
            src_ref=forward_out.at[2 * slot + part],
            dst_ref=forward_in.at[2 * slot + part],
            send_sem=forward_send.at[0],
            recv_sem=forward_recv.at[2 * slot + part],
            device_id={"slab": place},
            device_id_type=MESH,
        )

    def backward_copy(slot, part, place):
        return pltpu.make_async_remote_copy(
            src_ref=backward_out.at[2 * slot + part],
            dst_ref=backward_in.at[2 * slot + part],
            send_sem=backward_send.at[0],
            recv_sem=backward_recv.at[2 * slot + part],
            device_id={"slab": place},
            device_id_type=MESH,
        )

    def scaled(mixed, slot, side):
        scale = 1.0 / (grid[slot, 0:1] - rows[side])
        return (scale * mixed).astype(jnp.bfloat16)

    def count_in(state, slot, side):
        squared = state.astype(jnp.float32) ** 2
        part = jnp.sum(squared.reshape(-1, 8, orbitals), axis=0)
        density[side] += grid[slot, 1:2] * part

    def down(state, slot, side):
        mixed = dot(state, right_turned[side], NN)
        return dot(scaled(mixed, slot, side), left_turned[side], NN).astype(jnp.bfloat16)

    def up(state, slot, side):
        mixed = dot(state, left[side], NN)
        return dot(scaled(mixed, slot, side), right[side], NN).astype(jnp.bfloat16)

    def each(body):
        def step(slot, carry):
            body(slot)
            return carry

        lax.fori_loop(0, slots, step, 0)

    def parts(slot, body, order=(0, 1)):
        for part in order:
            if part:
                pl.when(slot < whole)(functools.partial(body, part))
            else:
                body(part)

    def near_end(side, refs, copy, close):
        def body(slot):
            pl.when(slot == count)(gift.wait_recv)
            fresh = close(scaled(first[...], slot, side)).astype(jnp.bfloat16)

            head = jnp.where(slot == count, fresh[half:], fresh[:half])
            pieces = (head, fresh[half:])

            def send(part):
                refs[2 * slot + part] = pieces[part]
                copy(slot, part, twin).start()

            parts(slot, send)
            parts(slot, lambda part: count_in(pieces[part], slot, side))

        each(body)
        start_swaps()

    def far_end(side, given, refs, copy, advance, place):
        def body(slot):
            pl.when(slot == count)(gift.wait_recv)

            def pass_on(part):
                copy(slot, part, twin).wait_recv()
                fresh = advance(given[2 * slot + part], slot, side)
                refs[2 * slot + part] = fresh
                copy(slot, part, place).start()
                count_in(fresh, slot, side)

            parts(slot, pass_on)

        each(body)

    @pl.when(spot == 0)
    def _():
        near_end(0, forward_out, forward_copy, lambda mixed: dot(mixed, left[0], NT))

    @pl.when(spot == 1)
    def _():
        far_end(1, forward_in, forward_out, forward_copy, down, 2)

    @pl.when(spot == chain - 1)
    def _():
        near_end(1, backward_out, backward_copy, lambda mixed: dot(mixed, right[1], NN))

    @pl.when(spot == chain - 2)
    def _():
        far_end(0, backward_in, backward_out, backward_copy, up, chain - 3)

    def sweep(given, refs, copy, bases, near, onward, count_rest):
        entry, link, exit_ = bases
        far = 1 - near

        def body(slot):
            pl.when(slot > 0)(lambda: count_rest(slot - 1))
            pl.when((slot == count) & inner)(gift.wait_recv)

            @pl.when(slot >= whole)
            def _():
                kept[half:] = jnp.zeros((half, orbitals), jnp.bfloat16)

            def advance(part):
                copy(slot, part, twin).wait_recv()
                near_mix = scaled(dot(given[2 * slot + part], entry[...], NN), slot, near)
                kept[part * half : (part + 1) * half] = near_mix
                far_mix = scaled(dot(near_mix, link[...], NN), slot, far)
                fresh = dot(far_mix, exit_[...], NN).astype(jnp.bfloat16)
                refs[2 * slot + part] = fresh
                pl.when(inner)(lambda: copy(slot, part, onward).start())
                count_in(fresh, slot, far)

            parts(slot, advance)

        each(body)

    def count_lower(slot):
        fresh = dot(kept[...], left_turned[0], NN).astype(jnp.bfloat16)
        count_in(fresh, slot, 0)

    def count_upper(slot):
        fresh = dot(kept[...], right[1], NN).astype(jnp.bfloat16)
        count_in(fresh, slot, 1)

    @pl.when((core == 0) & jnp.logical_not(lowest))
    def _():
        turn_bases(0)
        swap_rows.wait_recv()
        swap_right.wait_recv()
        joined[...] = dot(left_turned[0], right[1], NT).astype(jnp.bfloat16)
        swap_left.wait_recv()
        left_turned[1] = left[1].T
        sweep(
            forward_in, forward_out, forward_copy,
            (right_turned.at[0], joined, left_turned.at[1]), 0, spot + 2, count_lower,
        )

    @pl.when((core == 1) & jnp.logical_not(highest))
    def _():
        swap_rows.wait_recv()
        swap_left.wait_recv()
        joined[...] = dot(right[1], left[0], NN).astype(jnp.bfloat16)
        swap_right.wait_recv()
        sweep(
            backward_in, backward_out, backward_copy,
            (left.at[1], joined, right.at[0]), 1, spot - 2, count_upper,
        )

    def fold(side):
        return jnp.sum(density[side], axis=0, keepdims=True)

    hand_over = pltpu.make_async_remote_copy(
        src_ref=mine,
        dst_ref=extra,
        send_sem=extra_sem.at[0],
        recv_sem=extra_sem.at[0],
        device_id={"slab": twin},
        device_id_type=MESH,
    )

    def share(side, step):
        return pltpu.make_async_remote_copy(
            src_ref=partial.at[side],
            dst_ref=gathered.at[team],
            send_sem=gather_send.at[0],
            recv_sem=gather_recv.at[0],
            device_id={"energy": lax.rem(team + step, teams), "slab": 2 * chip + side},
            device_id_type=MESH,
        )

    def speak(side):
        partial[side] = fold(side) + extra[side]
        for step in range(1, teams):
            share(side, step).start()
        pl.when(core != side)(share(side, 0).start)

        @pl.when(core == side)
        def _():
            gathered[team] = partial[side]

    pl.when((core == 0) & inner)(lambda: count_lower(slots - 1))

    @pl.when(jnp.logical_not(speaks))
    def _():
        for side in range(2):
            mine[side] = fold(side)
        hand_over.start()

    @pl.when(speaks)
    def _():
        hand_over.wait_recv()

        @pl.when(highest)
        def _():
            speak(1)
            count_lower(slots - 1)
            speak(0)

        @pl.when(jnp.logical_not(highest))
        def _():
            speak(0)
            count_upper(slots - 1)
            speak(1)

    def sent(ref, sem):
        pltpu.make_async_remote_copy(
            src_ref=ref,
            dst_ref=ref,
            send_sem=sem,
            recv_sem=sem,
            device_id={"slab": twin},
            device_id_type=MESH,
        ).wait_send()

    def all_sent(refs, sem):
        pl.when(takes)(lambda: sent(refs.at[pl.ds(0, 2 * count + 1)], sem.at[0]))
        pl.when(gives)(lambda: sent(refs.at[pl.ds(0, 2 * count - 1)], sem.at[0]))
        pl.when(jnp.logical_not(takes | gives))(
            lambda: sent(refs.at[pl.ds(0, 2 * count)], sem.at[0])
        )

    pl.when(sends_forward | (spot == 0))(lambda: all_sent(forward_out, forward_send))
    pl.when(sends_backward | (spot == chain - 1))(
        lambda: all_sent(backward_out, backward_send)
    )

    @pl.when(inner | (spot == 0) | (spot == chain - 1))
    def _():
        swap_rows.wait_send()
        sent(left, swap_send.at[1])

    pl.when(jnp.logical_not(speaks))(hand_over.wait_send)
    pl.when(gives)(gift.wait_send)

    pl.when(speaks)(lambda: sent(gathered.at[pl.ds(0, 2 * teams - 1)], gather_send.at[0]))

    def received(members):
        ref = gathered.at[pl.ds(0, members)]
        pltpu.make_async_remote_copy(
            src_ref=ref,
            dst_ref=ref,
            send_sem=gather_send.at[0],
            recv_sem=gather_recv.at[0],
            device_id={"slab": twin},
            device_id_type=MESH,
        ).wait_recv()

    pl.when(jnp.logical_not(speaks))(lambda: received(teams))
    if teams > 1:
        pl.when(speaks)(lambda: received(teams - 1))
    total = gathered[0]
    for member in range(1, teams):
        total += gathered[member]
    out[...] = total


def local(
    teams,
    chain,
    left_basis,
    right_basis,
    potential_index,
    levels,
    energy_values,
    energy_weights,
    energy_index,
    left_source,
    right_source,
):
    count = energy_index.shape[0]
    orbitals = left_basis.shape[1]
    modes = left_source.shape[1]
    outside = pl.BlockSpec(memory_space=pltpu.HBM)
    square = pltpu.VMEM((2, orbitals, orbitals), jnp.bfloat16)
    block = pltpu.VMEM((2 * count + 1, modes // 2, orbitals), jnp.bfloat16)
    pieces = pltpu.SemaphoreType.DMA((2 * count + 1,))
    pair = pltpu.VMEM((2, 1, orbitals), jnp.float32)
    return pl.pallas_call(
        functools.partial(kernel, chain, teams),
        out_shape=pltpu.VMEM((1, orbitals), jnp.float32),
        in_specs=[pl.BlockSpec(memory_space=pltpu.SMEM)] + [outside] * 8,
        out_specs=pl.BlockSpec(memory_space=pltpu.VMEM),
        scratch_shapes=[
            pltpu.SMEM(energy_values.shape, jnp.float32),
            pltpu.SMEM(energy_weights.shape, jnp.float32),
            pltpu.SMEM(energy_index.shape, jnp.int32),
            pltpu.VMEM(levels.shape, jnp.float32),
            pltpu.VMEM(left_source.shape, jnp.bfloat16),
            square,
            square,
            square,
            square,
            pltpu.VMEM((orbitals, orbitals), jnp.bfloat16),
            pltpu.VMEM((count + 1, 2, orbitals), jnp.float32),
            pltpu.VMEM((2, 1, orbitals), jnp.float32),
            pltpu.VMEM((modes, orbitals), jnp.float32),
            pltpu.VMEM((modes, orbitals), jnp.bfloat16),
            pltpu.VMEM((2, 8, orbitals), jnp.float32),
            pair,
            pair,
            pair,
            pltpu.VMEM((2 * teams, 1, orbitals), jnp.float32),
            block,
            block,
            block,
            block,
            pltpu.SemaphoreType.DMA((7,)),
            pltpu.SemaphoreType.DMA((1,)),
            pltpu.SemaphoreType.DMA((2,)),
            pltpu.SemaphoreType.DMA((3,)),
            pltpu.SemaphoreType.DMA((1,)),
            pieces,
            pltpu.SemaphoreType.DMA((1,)),
            pieces,
            pltpu.SemaphoreType.DMA((1,)),
            pltpu.SemaphoreType.DMA((1,)),
            pltpu.SemaphoreType.DMA((1,)),
        ],
        compiler_params=pltpu.CompilerParams(
            collective_id=0, has_side_effects=True, vmem_limit_bytes=63 << 20
        ),
    )(
        potential_index,
        energy_values,
        energy_weights,
        energy_index,
        levels,
        left_source,
        right_source,
        left_basis,
        right_basis,
    )


def solution(mesh):
    placed = (
        P("slab", None, None),
        P("slab", None, None),
        P("slab"),
        P(),
        P(),
        P(),
        P("energy"),
        P(),
        P(),
    )
    return jax.shard_map(
        functools.partial(local, mesh.shape["energy"], mesh.shape["slab"]),
        mesh=mesh,
        in_specs=placed,
        out_specs=P("slab", None),
        check_vma=False,
    )
```

```python
import functools

import jax
import jax.numpy as jnp
from jax import lax
from jax.experimental import pallas as pl
from jax.experimental.pallas import tpu as pltpu
from jax.sharding import PartitionSpec as P

MESH = pl.DeviceIdType.MESH
NN = (((1,), (0,)), ((), ()))
NT = (((1,), (1,)), ((), ()))


def dot(a, b, dims):
    return lax.dot_general(a, b, dims, preferred_element_type=jnp.float32)


def kernel(
    chain,
    teams,
    potential,
    energies_hbm,
    weights_hbm,
    indices_hbm,
    levels_hbm,
    left_source_hbm,
    right_source_hbm,
    left_hbm,
    right_hbm,
    out,
    energies,
    weights,
    indices,
    levels,
    source,
    left,
    right,
    left_turned,
    right_turned,
    joined,
    grid,
    rows,
    first,
    kept,
    density,
    mine,
    extra,
    partial,
    gathered,
    forward_in,
    forward_out,
    backward_in,
    backward_out,
    load_sem,
    gift_sem,
    swap_send,
    swap_recv,
    forward_send,
    forward_recv,
    backward_send,
    backward_recv,
    extra_sem,
    gather_send,
    gather_recv,
):
    count = indices.shape[0]
    modes = source.shape[1]
    orbitals = levels.shape[1]
    half = modes // 2
    spot = lax.axis_index("slab")
    team = lax.axis_index("energy")
    chips = chain // 2
    chip = spot // 2
    core = spot % 2
    twin = spot + 1 - 2 * core
    lowest = chip == 0
    highest = chip == chips - 1
    inner = jnp.logical_not(lowest | highest)
    upper = chip >= chips // 2
    speaker = jnp.where(highest, 0, 1)
    speaks = core == speaker
    gives = (team == teams - 1) & (teams > 1)
    takes = (team == 0) & (teams > 1)
    slots = count + takes.astype(jnp.int32)
    whole = count - gives.astype(jnp.int32)

    def load(origin, target, place):
        return pltpu.make_async_copy(origin, target, load_sem.at[place])

    left_load = load(left_source_hbm, source, 0)
    right_load = load(right_source_hbm, source, 0)
    right_base = load(right_hbm.at[0], right.at[core], 1)
    left_base = load(left_hbm.at[0], left.at[core], 2)
    tables = [
        load(energies_hbm, energies, 3),
        load(weights_hbm, weights, 4),
        load(indices_hbm, indices, 5),
        load(levels_hbm, levels, 6),
    ]
    pl.when(spot == 0)(left_load.start)
    pl.when(spot == chain - 1)(right_load.start)
    left_base.start()
    for item in tables:
        item.start()
    right_base.start()

    barrier = pltpu.get_barrier_semaphore()

    def greet(place):
        pl.semaphore_signal(barrier, inc=1, device_id=place, device_id_type=MESH)

    greet({"slab": twin})
    pl.when((core == 0) & jnp.logical_not(lowest))(
        lambda: greet({"slab": jnp.where(chip == 1, 1, spot - 2)})
    )
    pl.when((core == 1) & jnp.logical_not(highest))(
        lambda: greet({"slab": jnp.where(chip == chips - 2, chain - 2, spot + 2)})
    )
    for step in range(1, teams):
        greet({"energy": lax.rem(team + step, teams), "slab": 2 * chip + speaker})
    pl.when(takes & jnp.logical_not(speaks))(lambda: greet({"energy": teams - 1}))
    sends_forward = jnp.where(lowest, core == 1, (core == 0) & jnp.logical_not(highest))
    sends_backward = jnp.where(highest, core == 0, (core == 1) & jnp.logical_not(lowest))
    greetings = (
        1
        + sends_forward.astype(jnp.int32)
        + sends_backward.astype(jnp.int32)
        + jnp.where(speaks, 2 * (teams - 1), gives.astype(jnp.int32))
    )

    density[...] = jnp.zeros_like(density)
    for item in tables:
        item.wait()
    rows[core] = levels[pl.ds(potential[0], 1), :]
    for slot in range(count):
        grid[slot, 0:1] = jnp.full((1, orbitals), energies[indices[slot]], jnp.float32)
        weight = weights[indices[slot]] / (count * teams * modes)
        grid[slot, 1:2] = jnp.full((1, orbitals), weight, jnp.float32)

    gift = pltpu.make_async_remote_copy(
        src_ref=grid.at[count - 1],
        dst_ref=grid.at[count],
        send_sem=gift_sem.at[0],
        recv_sem=gift_sem.at[0],
        device_id={"energy": 0},
        device_id_type=MESH,
    )

    def swap(origin, target, place):
        return pltpu.make_async_remote_copy(
            src_ref=origin,
            dst_ref=target,
            send_sem=swap_send.at[min(place, 1)],
            recv_sem=swap_recv.at[place],
            device_id={"slab": twin},
            device_id_type=MESH,
        )

    swap_rows = swap(rows.at[core], rows.at[core], 0)
    swap_right = swap(right_hbm.at[0], right.at[core], 1)
    swap_left = swap(left_hbm.at[0], left.at[core], 2)

    def start_swaps():
        swap_rows.start()

        @pl.when(core == 0)
        def _():
            swap_left.start()
            swap_right.start()

        @pl.when(core == 1)
        def _():
            swap_right.start()
            swap_left.start()

    def settle_bases():
        right_base.wait()
        left_base.wait()

    def turned_source():
        return source[...].astype(jnp.float32).T.astype(jnp.bfloat16)

    def turn_bases(side):
        left_turned[side] = left[side].T
        right_turned[side] = right[side].T

    @pl.when(spot == 0)
    def _():
        settle_bases()
        left_load.wait()
        first[...] = dot(turned_source(), right[0], NT)

    @pl.when(spot == chain - 1)
    def _():
        right_load.wait()
        left_base.wait()
        first[...] = dot(turned_source(), left[1], NN)
        right_base.wait()

    @pl.when(spot == 1)
    def _():
        settle_bases()
        turn_bases(1)

    pl.when(spot == chain - 2)(settle_bases)
    pl.semaphore_wait(barrier, greetings)
    pl.when(gives)(gift.start)

    @pl.when(inner)
    def _():
        start_swaps()
        settle_bases()

    def forward_copy(slot, part, place):
        return pltpu.make_async_remote_copy(
            src_ref=forward_out.at[2 * slot + part],
            dst_ref=forward_in.at[2 * slot + part],
            send_sem=forward_send.at[0],
            recv_sem=forward_recv.at[2 * slot + part],
            device_id={"slab": place},
            device_id_type=MESH,
        )

    def backward_copy(slot, part, place):
        return pltpu.make_async_remote_copy(
            src_ref=backward_out.at[2 * slot + part],
            dst_ref=backward_in.at[2 * slot + part],
            send_sem=backward_send.at[0],
            recv_sem=backward_recv.at[2 * slot + part],
            device_id={"slab": place},
            device_id_type=MESH,
        )

    def scaled(mixed, slot, side):
        scale = 1.0 / (grid[slot, 0:1] - rows[side])
        return (scale * mixed).astype(jnp.bfloat16)

    def count_in(state, slot, side):
        squared = state.astype(jnp.float32) ** 2
        part = jnp.sum(squared.reshape(-1, 8, orbitals), axis=0)
        density[side] += grid[slot, 1:2] * part

    def down(state, slot, side):
        mixed = dot(state, right_turned[side], NN)
        return dot(scaled(mixed, slot, side), left_turned[side], NN).astype(jnp.bfloat16)

    def up(state, slot, side):
        mixed = dot(state, left[side], NN)
        return dot(scaled(mixed, slot, side), right[side], NN).astype(jnp.bfloat16)

    def each(body):
        def step(slot, carry):
            body(slot)
            return carry

        lax.fori_loop(0, slots, step, 0)

    def parts(slot, body, order=(0, 1)):
        for part in order:
            if part:
                pl.when(slot < whole)(functools.partial(body, part))
            else:
                body(part)

    def near_end(side, refs, copy, close):
        def body(slot):
            pl.when(slot == count)(gift.wait_recv)
            fresh = close(scaled(first[...], slot, side)).astype(jnp.bfloat16)

            head = jnp.where(slot == count, fresh[half:], fresh[:half])
            pieces = (head, fresh[half:])

            def send(part):
                refs[2 * slot + part] = pieces[part]
                copy(slot, part, twin).start()

            parts(slot, send)
            parts(slot, lambda part: count_in(pieces[part], slot, side))

        each(body)
        start_swaps()

    def far_end(side, given, refs, copy, advance, place):
        def body(slot):
            pl.when(slot == count)(gift.wait_recv)

            def pass_on(part):
                copy(slot, part, twin).wait_recv()
                fresh = advance(given[2 * slot + part], slot, side)
                refs[2 * slot + part] = fresh
                copy(slot, part, place).start()
                count_in(fresh, slot, side)

            parts(slot, pass_on)

        each(body)

    @pl.when(spot == 0)
    def _():
        near_end(0, forward_out, forward_copy, lambda mixed: dot(mixed, left[0], NT))

    @pl.when(spot == 1)
    def _():
        far_end(1, forward_in, forward_out, forward_copy, down, 2)

    @pl.when(spot == chain - 1)
    def _():
        near_end(1, backward_out, backward_copy, lambda mixed: dot(mixed, right[1], NN))

    @pl.when(spot == chain - 2)
    def _():
        far_end(0, backward_in, backward_out, backward_copy, up, chain - 3)

    def sweep(given, refs, copy, bases, near, onward, count_rest):
        entry, link, exit_ = bases
        far = 1 - near
        spare = 2 * count + 1
        given[spare] = jnp.zeros((half, orbitals), jnp.bfloat16)

        def step(piece, carry):
            real = piece >= 0
            slot = jnp.maximum(piece, 0) // 2
            part = jnp.maximum(piece, 0) % 2
            place = jnp.where(real, piece, spare)
            pl.when((piece > 0) & (part == 0))(lambda: count_rest(slot - 1))
            pl.when((slot == count) & inner)(gift.wait_recv)

            @pl.when(slot >= whole)
            def _():
                kept[half:] = jnp.zeros((half, orbitals), jnp.bfloat16)

            pl.when(real)(lambda: copy(slot, part, twin).wait_recv())
            near_mix = scaled(dot(given[place], entry[...], NN), slot, near)
            kept[pl.ds(pl.multiple_of(part * half, half), half)] = near_mix
            far_mix = scaled(dot(near_mix, link[...], NN), slot, far)
            fresh = dot(far_mix, exit_[...], NN).astype(jnp.bfloat16)
            refs[place] = fresh
            pl.when(inner & real)(lambda: copy(slot, part, onward).start())
            count_in(fresh, slot, far)
            return carry

        lax.fori_loop(-1, slots + whole, step, 0)

    def count_lower(slot):
        fresh = dot(kept[...], left_turned[0], NN).astype(jnp.bfloat16)
        count_in(fresh, slot, 0)

    def count_upper(slot):
        fresh = dot(kept[...], right[1], NN).astype(jnp.bfloat16)
        count_in(fresh, slot, 1)

    @pl.when((core == 0) & jnp.logical_not(lowest))
    def _():
        turn_bases(0)
        swap_rows.wait_recv()
        swap_right.wait_recv()
        joined[...] = dot(left_turned[0], right[1], NT).astype(jnp.bfloat16)
        swap_left.wait_recv()
        left_turned[1] = left[1].T
        sweep(
            forward_in, forward_out, forward_copy,
            (right_turned.at[0], joined, left_turned.at[1]), 0, spot + 2, count_lower,
        )

    @pl.when((core == 1) & jnp.logical_not(highest))
    def _():
        swap_rows.wait_recv()
        swap_left.wait_recv()
        joined[...] = dot(right[1], left[0], NN).astype(jnp.bfloat16)
        swap_right.wait_recv()
        sweep(
            backward_in, backward_out, backward_copy,
            (left.at[1], joined, right.at[0]), 1, spot - 2, count_upper,
        )

    def fold(side):
        return jnp.sum(density[side], axis=0, keepdims=True)

    hand_over = pltpu.make_async_remote_copy(
        src_ref=mine,
        dst_ref=extra,
        send_sem=extra_sem.at[0],
        recv_sem=extra_sem.at[0],
        device_id={"slab": twin},
        device_id_type=MESH,
    )

    def share(side, step):
        return pltpu.make_async_remote_copy(
            src_ref=partial.at[side],
            dst_ref=gathered.at[team],
            send_sem=gather_send.at[0],
            recv_sem=gather_recv.at[0],
            device_id={"energy": lax.rem(team + step, teams), "slab": 2 * chip + side},
            device_id_type=MESH,
        )

    def speak(side):
        partial[side] = fold(side) + extra[side]
        for step in range(1, teams):
            share(side, step).start()
        pl.when(core != side)(share(side, 0).start)

        @pl.when(core == side)
        def _():
            gathered[team] = partial[side]

    pl.when((core == 0) & inner)(lambda: count_lower(slots - 1))

    @pl.when(jnp.logical_not(speaks))
    def _():
        for side in range(2):
            mine[side] = fold(side)
        hand_over.start()

    @pl.when(speaks)
    def _():
        hand_over.wait_recv()

        @pl.when(highest)
        def _():
            speak(1)
            count_lower(slots - 1)
            speak(0)

        @pl.when(jnp.logical_not(highest))
        def _():
            speak(0)
            count_upper(slots - 1)
            speak(1)

    def sent(ref, sem):
        pltpu.make_async_remote_copy(
            src_ref=ref,
            dst_ref=ref,
            send_sem=sem,
            recv_sem=sem,
            device_id={"slab": twin},
            device_id_type=MESH,
        ).wait_send()

    def all_sent(refs, sem):
        pl.when(takes)(lambda: sent(refs.at[pl.ds(0, 2 * count + 1)], sem.at[0]))
        pl.when(gives)(lambda: sent(refs.at[pl.ds(0, 2 * count - 1)], sem.at[0]))
        pl.when(jnp.logical_not(takes | gives))(
            lambda: sent(refs.at[pl.ds(0, 2 * count)], sem.at[0])
        )

    pl.when(sends_forward | (spot == 0))(lambda: all_sent(forward_out, forward_send))
    pl.when(sends_backward | (spot == chain - 1))(
        lambda: all_sent(backward_out, backward_send)
    )

    @pl.when(inner | (spot == 0) | (spot == chain - 1))
    def _():
        swap_rows.wait_send()
        sent(left, swap_send.at[1])

    pl.when(jnp.logical_not(speaks))(hand_over.wait_send)
    pl.when(gives)(gift.wait_send)

    pl.when(speaks)(lambda: sent(gathered.at[pl.ds(0, 2 * teams - 1)], gather_send.at[0]))

    def received(members):
        ref = gathered.at[pl.ds(0, members)]
        pltpu.make_async_remote_copy(
            src_ref=ref,
            dst_ref=ref,
            send_sem=gather_send.at[0],
            recv_sem=gather_recv.at[0],
            device_id={"slab": twin},
            device_id_type=MESH,
        ).wait_recv()

    pl.when(jnp.logical_not(speaks))(lambda: received(teams))
    if teams > 1:
        pl.when(speaks)(lambda: received(teams - 1))
    total = gathered[0]
    for member in range(1, teams):
        total += gathered[member]
    out[...] = total


def local(
    teams,
    chain,
    left_basis,
    right_basis,
    potential_index,
    levels,
    energy_values,
    energy_weights,
    energy_index,
    left_source,
    right_source,
):
    count = energy_index.shape[0]
    orbitals = left_basis.shape[1]
    modes = left_source.shape[1]
    outside = pl.BlockSpec(memory_space=pltpu.HBM)
    square = pltpu.VMEM((2, orbitals, orbitals), jnp.bfloat16)
    block = pltpu.VMEM((2 * count + 2, modes // 2, orbitals), jnp.bfloat16)
    pieces = pltpu.SemaphoreType.DMA((2 * count + 1,))
    pair = pltpu.VMEM((2, 1, orbitals), jnp.float32)
    return pl.pallas_call(
        functools.partial(kernel, chain, teams),
        out_shape=pltpu.VMEM((1, orbitals), jnp.float32),
        in_specs=[pl.BlockSpec(memory_space=pltpu.SMEM)] + [outside] * 8,
        out_specs=pl.BlockSpec(memory_space=pltpu.VMEM),
        scratch_shapes=[
            pltpu.SMEM(energy_values.shape, jnp.float32),
            pltpu.SMEM(energy_weights.shape, jnp.float32),
            pltpu.SMEM(energy_index.shape, jnp.int32),
            pltpu.VMEM(levels.shape, jnp.float32),
            pltpu.VMEM(left_source.shape, jnp.bfloat16),
            square,
            square,
            square,
            square,
            pltpu.VMEM((orbitals, orbitals), jnp.bfloat16),
            pltpu.VMEM((count + 1, 2, orbitals), jnp.float32),
            pltpu.VMEM((2, 1, orbitals), jnp.float32),
            pltpu.VMEM((modes, orbitals), jnp.float32),
            pltpu.VMEM((modes, orbitals), jnp.bfloat16),
            pltpu.VMEM((2, 8, orbitals), jnp.float32),
            pair,
            pair,
            pair,
            pltpu.VMEM((2 * teams, 1, orbitals), jnp.float32),
            block,
            block,
            block,
            block,
            pltpu.SemaphoreType.DMA((7,)),
            pltpu.SemaphoreType.DMA((1,)),
            pltpu.SemaphoreType.DMA((2,)),
            pltpu.SemaphoreType.DMA((3,)),
            pltpu.SemaphoreType.DMA((1,)),
            pieces,
            pltpu.SemaphoreType.DMA((1,)),
            pieces,
            pltpu.SemaphoreType.DMA((1,)),
            pltpu.SemaphoreType.DMA((1,)),
            pltpu.SemaphoreType.DMA((1,)),
        ],
        compiler_params=pltpu.CompilerParams(
            collective_id=0, has_side_effects=True, vmem_limit_bytes=63 << 20
        ),
    )(
        potential_index,
        energy_values,
        energy_weights,
        energy_index,
        levels,
        left_source,
        right_source,
        left_basis,
        right_basis,
    )


def solution(mesh):
    placed = (
        P("slab", None, None),
        P("slab", None, None),
        P("slab"),
        P(),
        P(),
        P(),
        P("energy"),
        P(),
        P(),
    )
    return jax.shard_map(
        functools.partial(local, mesh.shape["energy"], mesh.shape["slab"]),
        mesh=mesh,
        in_specs=placed,
        out_specs=P("slab", None),
        check_vma=False,
    )
```

```python
import functools

import jax
import jax.numpy as jnp
from jax import lax
from jax.experimental import pallas as pl
from jax.experimental.pallas import tpu as pltpu
from jax.sharding import PartitionSpec as P

MESH = pl.DeviceIdType.MESH
NN = (((1,), (0,)), ((), ()))
NT = (((1,), (1,)), ((), ()))


def dot(a, b, dims):
    return lax.dot_general(a, b, dims, preferred_element_type=jnp.float32)


def kernel(
    chain,
    teams,
    potential,
    energies_hbm,
    weights_hbm,
    indices_hbm,
    levels_hbm,
    left_source_hbm,
    right_source_hbm,
    left_hbm,
    right_hbm,
    out,
    energies,
    weights,
    indices,
    levels,
    source,
    left,
    right,
    left_turned,
    right_turned,
    joined,
    grid,
    rows,
    first,
    kept,
    density,
    mine,
    extra,
    partial,
    gathered,
    forward_in,
    forward_out,
    backward_in,
    backward_out,
    load_sem,
    gift_sem,
    swap_send,
    swap_recv,
    forward_send,
    forward_recv,
    backward_send,
    backward_recv,
    extra_sem,
    gather_send,
    gather_recv,
):
    count = indices.shape[0]
    modes = source.shape[1]
    orbitals = levels.shape[1]
    half = modes // 2
    spot = lax.axis_index("slab")
    team = lax.axis_index("energy")
    chips = chain // 2
    chip = spot // 2
    core = spot % 2
    twin = spot + 1 - 2 * core
    lowest = chip == 0
    highest = chip == chips - 1
    inner = jnp.logical_not(lowest | highest)
    upper = chip >= chips // 2
    speaker = jnp.where(highest, 0, 1)
    speaks = core == speaker
    gives = (team == teams - 1) & (teams > 1)
    takes = (team == 0) & (teams > 1)
    slots = count + takes.astype(jnp.int32)
    whole = count - gives.astype(jnp.int32)

    def load(origin, target, place):
        return pltpu.make_async_copy(origin, target, load_sem.at[place])

    left_load = load(left_source_hbm, source, 0)
    right_load = load(right_source_hbm, source, 0)
    right_base = load(right_hbm.at[0], right.at[core], 1)
    left_base = load(left_hbm.at[0], left.at[core], 2)
    tables = [
        load(energies_hbm, energies, 3),
        load(weights_hbm, weights, 4),
        load(indices_hbm, indices, 5),
        load(levels_hbm, levels, 6),
    ]
    pl.when(spot == 0)(left_load.start)
    pl.when(spot == chain - 1)(right_load.start)
    left_base.start()
    for item in tables:
        item.start()
    right_base.start()

    barrier = pltpu.get_barrier_semaphore()

    def greet(place):
        pl.semaphore_signal(barrier, inc=1, device_id=place, device_id_type=MESH)

    greet({"slab": twin})
    pl.when((core == 0) & jnp.logical_not(lowest))(
        lambda: greet({"slab": jnp.where(chip == 1, 1, spot - 2)})
    )
    pl.when((core == 1) & jnp.logical_not(highest))(
        lambda: greet({"slab": jnp.where(chip == chips - 2, chain - 2, spot + 2)})
    )
    for step in range(1, teams):
        greet({"energy": lax.rem(team + step, teams), "slab": 2 * chip + speaker})
    pl.when(takes & jnp.logical_not(speaks))(lambda: greet({"energy": teams - 1}))
    sends_forward = jnp.where(lowest, core == 1, (core == 0) & jnp.logical_not(highest))
    sends_backward = jnp.where(highest, core == 0, (core == 1) & jnp.logical_not(lowest))
    greetings = (
        1
        + sends_forward.astype(jnp.int32)
        + sends_backward.astype(jnp.int32)
        + jnp.where(speaks, 2 * (teams - 1), gives.astype(jnp.int32))
    )

    density[...] = jnp.zeros_like(density)
    for item in tables:
        item.wait()
    rows[core] = levels[pl.ds(potential[0], 1), :]
    for slot in range(count):
        grid[slot, 0:1] = jnp.full((1, orbitals), energies[indices[slot]], jnp.float32)
        weight = weights[indices[slot]] / (count * teams * modes)
        grid[slot, 1:2] = jnp.full((1, orbitals), weight, jnp.float32)

    gift = pltpu.make_async_remote_copy(
        src_ref=grid.at[count - 1],
        dst_ref=grid.at[count],
        send_sem=gift_sem.at[0],
        recv_sem=gift_sem.at[0],
        device_id={"energy": 0},
        device_id_type=MESH,
    )

    def swap(origin, target, place):
        return pltpu.make_async_remote_copy(
            src_ref=origin,
            dst_ref=target,
            send_sem=swap_send.at[min(place, 1)],
            recv_sem=swap_recv.at[place],
            device_id={"slab": twin},
            device_id_type=MESH,
        )

    swap_rows = swap(rows.at[core], rows.at[core], 0)
    swap_right = swap(right_hbm.at[0], right.at[core], 1)
    swap_left = swap(left_hbm.at[0], left.at[core], 2)

    def start_swaps():
        swap_rows.start()

        @pl.when(core == 0)
        def _():
            swap_left.start()
            swap_right.start()

        @pl.when(core == 1)
        def _():
            swap_right.start()
            swap_left.start()

    def settle_bases():
        right_base.wait()
        left_base.wait()

    def turned_source():
        return source[...].astype(jnp.float32).T.astype(jnp.bfloat16)

    def turn_bases(side):
        left_turned[side] = left[side].T
        right_turned[side] = right[side].T

    @pl.when(spot == 0)
    def _():
        settle_bases()
        left_load.wait()
        first[...] = dot(turned_source(), right[0], NT)

    @pl.when(spot == chain - 1)
    def _():
        right_load.wait()
        left_base.wait()
        first[...] = dot(turned_source(), left[1], NN)
        right_base.wait()

    @pl.when(spot == 1)
    def _():
        settle_bases()
        turn_bases(1)

    pl.when(spot == chain - 2)(settle_bases)
    pl.semaphore_wait(barrier, greetings)
    pl.when(gives)(gift.start)

    @pl.when(inner)
    def _():
        start_swaps()
        settle_bases()

    def forward_copy(slot, part, place):
        return pltpu.make_async_remote_copy(
            src_ref=forward_out.at[2 * slot + part],
            dst_ref=forward_in.at[2 * slot + part],
            send_sem=forward_send.at[0],
            recv_sem=forward_recv.at[2 * slot + part],
            device_id={"slab": place},
            device_id_type=MESH,
        )

    def backward_copy(slot, part, place):
        return pltpu.make_async_remote_copy(
            src_ref=backward_out.at[2 * slot + part],
            dst_ref=backward_in.at[2 * slot + part],
            send_sem=backward_send.at[0],
            recv_sem=backward_recv.at[2 * slot + part],
            device_id={"slab": place},
            device_id_type=MESH,
        )

    def scaled(mixed, slot, side):
        scale = 1.0 / (grid[slot, 0:1] - rows[side])
        return (scale * mixed).astype(jnp.bfloat16)

    def count_in(state, slot, side):
        squared = state.astype(jnp.float32) ** 2
        part = jnp.sum(squared.reshape(-1, 8, orbitals), axis=0)
        density[side] += grid[slot, 1:2] * part

    def down(state, slot, side):
        mixed = dot(state, right_turned[side], NN)
        return dot(scaled(mixed, slot, side), left_turned[side], NN).astype(jnp.bfloat16)

    def up(state, slot, side):
        mixed = dot(state, left[side], NN)
        return dot(scaled(mixed, slot, side), right[side], NN).astype(jnp.bfloat16)

    def each(body):
        def step(slot, carry):
            body(slot)
            return carry

        lax.fori_loop(0, slots, step, 0)

    def parts(slot, body, order=(0, 1)):
        for part in order:
            if part:
                pl.when(slot < whole)(functools.partial(body, part))
            else:
                body(part)

    def near_end(side, refs, copy, close):
        def body(slot):
            pl.when(slot == count)(gift.wait_recv)
            fresh = close(scaled(first[...], slot, side)).astype(jnp.bfloat16)

            head = jnp.where(slot == count, fresh[half:], fresh[:half])
            pieces = (head, fresh[half:])

            def send(part):
                refs[2 * slot + part] = pieces[part]
                copy(slot, part, twin).start()

            parts(slot, send)
            parts(slot, lambda part: count_in(pieces[part], slot, side))

        each(body)
        start_swaps()

    spare = 2 * count + 1

    def far_end(side, given, refs, copy, advance, onward):
        def step(piece, carry):
            slot = piece // 2
            part = piece % 2
            pl.when(slot == count)(gift.wait_recv)
            copy(slot, part, twin).wait_recv()
            fresh = advance(given[piece], slot, side)
            refs[piece] = fresh
            copy(slot, part, onward).start()
            count_in(fresh, slot, side)
            return carry

        lax.fori_loop(0, slots + whole, step, 0)

    @pl.when(spot == 0)
    def _():
        near_end(0, forward_out, forward_copy, lambda mixed: dot(mixed, left[0], NT))

    @pl.when(spot == 1)
    def _():
        far_end(1, forward_in, forward_out, forward_copy, down, 2)

    @pl.when(spot == chain - 1)
    def _():
        near_end(1, backward_out, backward_copy, lambda mixed: dot(mixed, right[1], NN))

    @pl.when(spot == chain - 2)
    def _():
        far_end(0, backward_in, backward_out, backward_copy, up, chain - 3)

    def sweep(given, refs, copy, bases, near, onward, count_rest):
        entry, link, exit_ = bases
        far = 1 - near
        given[spare] = jnp.zeros((half, orbitals), jnp.bfloat16)

        def step(piece, carry):
            real = piece >= 0
            slot = jnp.maximum(piece, 0) // 2
            part = jnp.maximum(piece, 0) % 2
            place = jnp.where(real, piece, spare)
            pl.when((piece > 0) & (part == 0))(lambda: count_rest(slot - 1))
            pl.when((slot == count) & inner)(gift.wait_recv)

            @pl.when(slot >= whole)
            def _():
                kept[half:] = jnp.zeros((half, orbitals), jnp.bfloat16)

            pl.when(real)(lambda: copy(slot, part, twin).wait_recv())
            near_mix = scaled(dot(given[place], entry[...], NN), slot, near)
            kept[pl.ds(pl.multiple_of(part * half, half), half)] = near_mix
            far_mix = scaled(dot(near_mix, link[...], NN), slot, far)
            fresh = dot(far_mix, exit_[...], NN).astype(jnp.bfloat16)
            refs[place] = fresh
            pl.when(inner & real)(lambda: copy(slot, part, onward).start())
            count_in(fresh, slot, far)
            return carry

        lax.fori_loop(-1, slots + whole, step, 0)

    def count_lower(slot):
        fresh = dot(kept[...], left_turned[0], NN).astype(jnp.bfloat16)
        count_in(fresh, slot, 0)

    def count_upper(slot):
        fresh = dot(kept[...], right[1], NN).astype(jnp.bfloat16)
        count_in(fresh, slot, 1)

    @pl.when((core == 0) & jnp.logical_not(lowest))
    def _():
        turn_bases(0)
        swap_rows.wait_recv()
        swap_right.wait_recv()
        joined[...] = dot(left_turned[0], right[1], NT).astype(jnp.bfloat16)
        swap_left.wait_recv()
        left_turned[1] = left[1].T
        sweep(
            forward_in, forward_out, forward_copy,
            (right_turned.at[0], joined, left_turned.at[1]), 0, spot + 2, count_lower,
        )

    @pl.when((core == 1) & jnp.logical_not(highest))
    def _():
        swap_rows.wait_recv()
        swap_left.wait_recv()
        joined[...] = dot(right[1], left[0], NN).astype(jnp.bfloat16)
        swap_right.wait_recv()
        sweep(
            backward_in, backward_out, backward_copy,
            (left.at[1], joined, right.at[0]), 1, spot - 2, count_upper,
        )

    def fold(side):
        return jnp.sum(density[side], axis=0, keepdims=True)

    hand_over = pltpu.make_async_remote_copy(
        src_ref=mine,
        dst_ref=extra,
        send_sem=extra_sem.at[0],
        recv_sem=extra_sem.at[0],
        device_id={"slab": twin},
        device_id_type=MESH,
    )

    def share(side, step):
        return pltpu.make_async_remote_copy(
            src_ref=partial.at[side],
            dst_ref=gathered.at[team],
            send_sem=gather_send.at[0],
            recv_sem=gather_recv.at[0],
            device_id={"energy": lax.rem(team + step, teams), "slab": 2 * chip + side},
            device_id_type=MESH,
        )

    def speak(side):
        partial[side] = fold(side) + extra[side]
        for step in reversed(range(1, teams)):
            share(side, step).start()
        pl.when(core != side)(share(side, 0).start)

        @pl.when(core == side)
        def _():
            gathered[team] = partial[side]

    pl.when((core == 0) & inner)(lambda: count_lower(slots - 1))

    @pl.when(jnp.logical_not(speaks))
    def _():
        for side in range(2):
            mine[side] = fold(side)
        hand_over.start()

    @pl.when(speaks)
    def _():
        hand_over.wait_recv()

        @pl.when(highest)
        def _():
            speak(1)
            count_lower(slots - 1)
            speak(0)

        @pl.when(jnp.logical_not(highest))
        def _():
            speak(0)
            count_upper(slots - 1)
            speak(1)

    def sent(ref, sem):
        pltpu.make_async_remote_copy(
            src_ref=ref,
            dst_ref=ref,
            send_sem=sem,
            recv_sem=sem,
            device_id={"slab": twin},
            device_id_type=MESH,
        ).wait_send()

    def all_sent(refs, sem):
        pl.when(takes)(lambda: sent(refs.at[pl.ds(0, 2 * count + 1)], sem.at[0]))
        pl.when(gives)(lambda: sent(refs.at[pl.ds(0, 2 * count - 1)], sem.at[0]))
        pl.when(jnp.logical_not(takes | gives))(
            lambda: sent(refs.at[pl.ds(0, 2 * count)], sem.at[0])
        )

    pl.when(sends_forward | (spot == 0))(lambda: all_sent(forward_out, forward_send))
    pl.when(sends_backward | (spot == chain - 1))(
        lambda: all_sent(backward_out, backward_send)
    )

    @pl.when(inner | (spot == 0) | (spot == chain - 1))
    def _():
        swap_rows.wait_send()
        sent(left, swap_send.at[1])

    pl.when(jnp.logical_not(speaks))(hand_over.wait_send)
    pl.when(gives)(gift.wait_send)

    pl.when(speaks)(lambda: sent(gathered.at[pl.ds(0, 2 * teams - 1)], gather_send.at[0]))

    def received(members):
        ref = gathered.at[pl.ds(0, members)]
        pltpu.make_async_remote_copy(
            src_ref=ref,
            dst_ref=ref,
            send_sem=gather_send.at[0],
            recv_sem=gather_recv.at[0],
            device_id={"slab": twin},
            device_id_type=MESH,
        ).wait_recv()

    pl.when(jnp.logical_not(speaks))(lambda: received(teams))
    if teams > 1:
        pl.when(speaks)(lambda: received(teams - 1))
    total = gathered[0]
    for member in range(1, teams):
        total += gathered[member]
    out[...] = total


def local(
    teams,
    chain,
    left_basis,
    right_basis,
    potential_index,
    levels,
    energy_values,
    energy_weights,
    energy_index,
    left_source,
    right_source,
):
    count = energy_index.shape[0]
    orbitals = left_basis.shape[1]
    modes = left_source.shape[1]
    outside = pl.BlockSpec(memory_space=pltpu.HBM)
    square = pltpu.VMEM((2, orbitals, orbitals), jnp.bfloat16)
    block = pltpu.VMEM((2 * count + 2, modes // 2, orbitals), jnp.bfloat16)
    pieces = pltpu.SemaphoreType.DMA((2 * count + 1,))
    pair = pltpu.VMEM((2, 1, orbitals), jnp.float32)
    return pl.pallas_call(
        functools.partial(kernel, chain, teams),
        out_shape=pltpu.VMEM((1, orbitals), jnp.float32),
        in_specs=[pl.BlockSpec(memory_space=pltpu.SMEM)] + [outside] * 8,
        out_specs=pl.BlockSpec(memory_space=pltpu.VMEM),
        scratch_shapes=[
            pltpu.SMEM(energy_values.shape, jnp.float32),
            pltpu.SMEM(energy_weights.shape, jnp.float32),
            pltpu.SMEM(energy_index.shape, jnp.int32),
            pltpu.VMEM(levels.shape, jnp.float32),
            pltpu.VMEM(left_source.shape, jnp.bfloat16),
            square,
            square,
            square,
            square,
            pltpu.VMEM((orbitals, orbitals), jnp.bfloat16),
            pltpu.VMEM((count + 1, 2, orbitals), jnp.float32),
            pltpu.VMEM((2, 1, orbitals), jnp.float32),
            pltpu.VMEM((modes, orbitals), jnp.float32),
            pltpu.VMEM((modes, orbitals), jnp.bfloat16),
            pltpu.VMEM((2, 8, orbitals), jnp.float32),
            pair,
            pair,
            pair,
            pltpu.VMEM((2 * teams, 1, orbitals), jnp.float32),
            block,
            block,
            block,
            block,
            pltpu.SemaphoreType.DMA((7,)),
            pltpu.SemaphoreType.DMA((1,)),
            pltpu.SemaphoreType.DMA((2,)),
            pltpu.SemaphoreType.DMA((3,)),
            pltpu.SemaphoreType.DMA((1,)),
            pieces,
            pltpu.SemaphoreType.DMA((1,)),
            pieces,
            pltpu.SemaphoreType.DMA((1,)),
            pltpu.SemaphoreType.DMA((1,)),
            pltpu.SemaphoreType.DMA((1,)),
        ],
        compiler_params=pltpu.CompilerParams(
            collective_id=0, has_side_effects=True, vmem_limit_bytes=63 << 20
        ),
    )(
        potential_index,
        energy_values,
        energy_weights,
        energy_index,
        levels,
        left_source,
        right_source,
        left_basis,
        right_basis,
    )


def solution(mesh):
    placed = (
        P("slab", None, None),
        P("slab", None, None),
        P("slab"),
        P(),
        P(),
        P(),
        P("energy"),
        P(),
        P(),
    )
    return jax.shard_map(
        functools.partial(local, mesh.shape["energy"], mesh.shape["slab"]),
        mesh=mesh,
        in_specs=placed,
        out_specs=P("slab", None),
        check_vma=False,
    )
```
